512 devices in a mesh: nodes: 128 (over y, z, core), feat: 4 (over x).
Axes of the slice: x: 4, y: 8, z: 8, core: 2. Of those that a mesh axis runs over, the one named last changes fastest.
Arguments:
- feats: bfloat16 [1536, 4, 8192], P('nodes', 'feat'), may hold values from -120 to 120
- w_qkv: bfloat16 [256, 768], P(None, 'feat'), may hold values from -0.375 to 0.375
- w_gcn: bfloat16 [256, 256], P(None, 'feat'), may hold values from -0.375 to 0.375
- nbr_owner: int32 [1536, 4], P('nodes'), may hold values from 0 to 127, all different within a row; in each aligned block of 12 rows (0 to 11, 12 to 23, ...) at most 2 rows name the same one
- nbr_tile: int32 [1536, 4], P('nodes'), may hold values from 0 to 11
- adj_blocks: bfloat16 [1536, 4, 128, 128], P('nodes', 'feat'), may hold values from -0.25 to 0.25
- grad_out: bfloat16 [1536, 4, 8192], P('nodes', 'feat'), may hold values from -6 to 6
Outputs:
- mixed: bfloat16 [1536, 4, 8192], P('nodes', 'feat')
- grad_x: bfloat16 [1536, 4, 8192], P('nodes', 'feat')
- grad_qkv: float32 [256, 768], P(None, 'feat')
- grad_gcn: float32 [256, 256], P(None, 'feat')
The draws below stay inside these ranges and needn't reach their ends.
Inputs may be any that keep to these rules, and one draw needn't show every extreme that they name: `nbr_owner`: the 4 owners listed for one tile differ; the 12 tiles of one partition list one owner at most 2 times, and some partition lists some owner exactly 2 times.
All inputs are finite; a program needn't handle non-finite values.
Results may differ from the reference program's by a relative error of at most 0.012.
Values may be sent and summed in bfloat16 or wider, within the bound.
A program may use at most 64 MiB of HBM per device.

```python
import math
import jax
import jax.numpy as jnp
import numpy as np
from jax import lax

D = 256
HEADS = 4
HD = 64
TILE = 128
TB = 12
NB = 4
CAP = 2
TILES = 1536
ROWS = 196608
N_NODES = 128


def draw_feats(key, part):
    key_rows, key_cols, key_means, key_base = jax.random.split(key, 4)
    row_count = ROWS
    position = jnp.arange(row_count, dtype=jnp.float32) / row_count
    row_scale = jnp.exp(jnp.log(3.0) * position + jax.random.uniform(key_rows, (row_count,), jnp.float32, -1.15, 1.15))
    col_scale = jnp.exp(jax.random.uniform(key_cols, (D,), jnp.float32, jnp.log(0.3), jnp.log(3.0)))
    tile_means = jnp.clip(jax.random.normal(key_means, (row_count // TILE, D), jnp.float32) * 0.7, -3.0, 3.0)
    region = jnp.repeat(tile_means, TILE, axis=0)
    base = jnp.clip(jax.random.normal(key_base, (row_count, D), jnp.float32), -5.0, 5.0)
    rows_matrix = (base + region) * row_scale[:, None] * col_scale[None, :] * 0.5
    return rows_matrix.reshape(TILES, TILE, HEADS, HD).transpose(0, 2, 1, 3).reshape(TILES, HEADS, TILE * HD).astype(jnp.bfloat16)


def touch_ends(values, key, low, high):
    longest = values.shape.index(max(values.shape))
    spots = []
    for shift in (0, 1):
        where = [jax.random.randint(jax.random.fold_in(key, axis), (), 0, length) for axis, length in enumerate(values.shape)]
        where[longest] = (where[longest] + shift) % values.shape[longest]
        spots.append(tuple(where))
    return values.at[spots[0]].set(low).at[spots[1]].set(high)


def steps_of(stream_key, extent, cuts, smallest, high):
    loudness = 1.0
    for dim, shards_of in cuts:
        draws = jax.random.uniform(jax.random.fold_in(jax.random.fold_in(stream_key, 6), dim), (shards_of,), jnp.float32, smallest / len(cuts), high / len(cuts))
        loudness = loudness * jnp.repeat(jnp.exp(draws), extent[dim] // shards_of).reshape((-1,) + (1,) * (len(extent) - 1 - dim))
    return loudness


def shared_out(own_key, own, number, rows, number_of, top, limit, lean):
    sequence = jax.random.permutation(own_key, number_of)
    packed, usual = load_shares(number_of, rows * top, limit, lean, True), load_shares(number_of, rows * top, limit, lean, False)
    places = jnp.arange(number_of)

    def named(sizes, turn):
        used = int((sizes > 0).sum())
        fixed = max(1, used // 4)
        shifted = fixed + (places - fixed + turn * (used - fixed)) % max(1, number_of - fixed)
        return jnp.zeros((number_of,), jnp.int32).at[sequence[jnp.where(places < fixed, places, shifted)]].set(jnp.asarray(sizes, jnp.int32))

    sizes = jnp.where(number % 4 == 0, named(packed, number // 4), named(usual, number - number // 4 - 1))
    mixed = jax.random.permutation(jax.random.fold_in(own, 3), number_of)
    donor, receiver = mixed[0:number_of // 2 * 2:2], mixed[1:number_of // 2 * 2:2]
    margin = jnp.minimum(sizes[donor] - 1, limit - sizes[receiver]) // 2
    margin = jnp.where((donor == sequence[0]) | (receiver == sequence[0]) | (sizes[receiver] == 0), 0, jnp.maximum(margin, 0))
    shifted = jax.random.randint(jax.random.fold_in(own, 4), (number_of // 2,), 0, 1 << 20) % (margin + 1)
    sizes = sizes.at[donor].add(-shifted).at[receiver].add(shifted)
    labels = jnp.searchsorted(jnp.cumsum(sizes), jnp.arange(rows * top), side="right").astype(jnp.int32)
    table = labels.reshape(top, rows).T
    table = table[jax.random.permutation(jax.random.fold_in(own, 1), rows)]
    turn = jax.random.randint(jax.random.fold_in(own, 2), (rows, 1), 0, top)
    return jnp.take_along_axis(table, (jnp.arange(top)[None, :] + turn) % top, axis=1)


def load_shares(count, total, most, skew, full):
    portions = [(1 << 20) // math.isqrt(grade ** skew) + 1 for grade in range(1, count + 1)]
    largest = most if full else min(most, max(-(-total // count), total * portions[0] // sum(portions)))
    least = 1 if total - largest >= count - 1 else 0
    holding, spare = [largest] + [least] * (count - 1), total - largest - least * (count - 1)
    while spare > 0:
        movable = [i for i in range(1, count) if holding[i] < largest] or [i for i in range(1, count) if holding[i] < most]
        pool, budget = sum([portions[i] for i in movable]), spare
        for i in movable:
            more = min(most - holding[i], max(1, budget * portions[i] // pool), spare)
            holding[i] = holding[i] + more
            spare = spare - more
    return np.array(holding)


def bell_draw(own_key, shape, spread, reach, shards=(), kind=jnp.bfloat16):
    gain = steps_of(own_key, shape, shards, -0.22, 0.18) if shards else 1.0
    result = jax.random.normal(own_key, shape, jnp.float32) * spread * gain
    return jnp.minimum(jnp.maximum(result, -reach), reach).astype(kind)


def setup_inputs(seed: int = 0) -> dict:
    splits = jax.random.split(jax.random.key(seed), 8)
    feats = draw_feats(jax.random.fold_in(splits[7], 71), 0)
    w_qkv = bell_draw(splits[1], (D, 3 * D), D ** -0.5, 0.375, ((1, 4),))
    w_gcn = bell_draw(splits[2], (D, D), D ** -0.5, 0.375, ((1, 4),))
    nbr_owner_keys = jax.random.split(jax.random.fold_in(splits[3], 1), TILES // TB)
    nbr_owner_turns = jax.random.permutation(jax.random.fold_in(splits[3], 3), TILES // TB)
    nbr_owner = jax.vmap(lambda own, number: shared_out(jax.random.fold_in(splits[3], 2), own, number, TB, N_NODES, NB, CAP, 2))(nbr_owner_keys, nbr_owner_turns).reshape((TILES, NB))
    nbr_tile = touch_ends(jax.random.randint(splits[4], (TILES, NB), 0, TB), jax.random.fold_in(splits[4], 1), 0, TB - 1).astype(jnp.int32)
    adj_blocks = bell_draw(splits[5], (TILES, NB, TILE, TILE), (TILE * NB) ** -0.5, 0.25, ((0, 128), (1, 4)))
    grad_out = bell_draw(splits[6], (TILES, HEADS, TILE * HD), 1.0, 6.0, ((0, 128), (1, 4)))
    return {"feats": feats, "w_qkv": w_qkv, "w_gcn": w_gcn, "nbr_owner": nbr_owner, "nbr_tile": nbr_tile, "adj_blocks": adj_blocks, "grad_out": grad_out}


epsilon = 1e-06

def to_rows(tiled):
    return tiled.reshape(TILES, HEADS, TILE, HD).transpose(0, 2, 1, 3).reshape(ROWS, D)

def to_tiles(rows_matrix):
    return rows_matrix.reshape(TILES, TILE, HEADS, HD).transpose(0, 2, 1, 3).reshape(TILES, HEADS, TILE * HD)

def neighbour_sum(y_tiles, adj_groups, id_groups):

    def one_group(pair):
        blocks, ids = pair
        fetched = y_tiles[ids].astype(jnp.float32)
        return jnp.einsum('tnab,tnbh->tah', blocks.astype(jnp.float32), fetched)
    return lax.map(one_group, (adj_groups, id_groups))

def spread_back(start_acc, adj_groups, id_groups, grad_groups):

    def one_group(acc, triple):
        blocks, ids, grad_tile = triple
        contrib = jnp.einsum('tnab,tah->tnbh', blocks.astype(jnp.float32), grad_tile.astype(jnp.float32))
        contrib = lax.optimization_barrier(contrib.astype(jnp.bfloat16)).astype(jnp.float32)
        acc = acc.at[ids.reshape(-1)].add(contrib.reshape(-1, TILE, D))
        return (acc, None)
    final_acc, _ = lax.scan(one_group, start_acc, (adj_groups, id_groups, grad_groups))
    return final_acc

def reference(feats, w_qkv, w_gcn, nbr_owner, nbr_tile, adj_blocks, grad_out):
    x_rows = to_rows(feats)
    g_rows = to_rows(grad_out)
    row_count = x_rows.shape[0]
    proj = jnp.dot(x_rows, w_qkv, preferred_element_type=jnp.float32).astype(jnp.bfloat16)
    proj = proj.reshape(row_count, HEADS, 3, HD)
    query_full = proj[:, :, 0].astype(jnp.float32)
    key_full = proj[:, :, 1].astype(jnp.float32)
    value_full = proj[:, :, 2].astype(jnp.float32)
    sq_sum = lax.optimization_barrier(jnp.sum(query_full * query_full, axis=(0, 2)))
    sk_sum = lax.optimization_barrier(jnp.sum(key_full * key_full, axis=(0, 2)))
    kv_state = jnp.einsum('nhe,nhf->hef', key_full, value_full)
    attn_scale = jnp.sqrt(jnp.float32(row_count)) / jnp.sqrt(sq_sum * sk_sum + epsilon)
    mix_rows = jnp.einsum('nhe,hef->nhf', query_full, kv_state, precision=lax.Precision.HIGHEST)
    y_rows = jnp.dot(x_rows, w_gcn, preferred_element_type=jnp.float32).astype(jnp.bfloat16)
    tile_ids = (nbr_owner * TB + nbr_tile).astype(jnp.int32).reshape(N_NODES, TB, NB)
    adj_groups = adj_blocks.reshape(N_NODES, TB, NB, TILE, TILE)
    y_tiles = y_rows.reshape(TILES, TILE, D)
    gcn_sum = neighbour_sum(y_tiles, adj_groups, tile_ids).reshape(row_count, D)
    gcn_rows = y_rows.astype(jnp.float32) + gcn_sum
    attn_rows = value_full + attn_scale[None, :, None] * mix_rows
    mixed = to_tiles((attn_rows.reshape(row_count, D) + gcn_rows).astype(jnp.bfloat16))
    grad_full = g_rows.astype(jnp.float32).reshape(row_count, HEADS, HD)
    pq_state = jnp.einsum('nhe,nhf->hef', query_full, grad_full)
    scale_grad = jnp.einsum('nhf,nhf->h', grad_full, mix_rows)
    dm_state = attn_scale[:, None, None] * pq_state
    denominator = sq_sum * sk_sum + epsilon
    gq_coef = -0.5 * scale_grad * attn_scale * sk_sum / denominator
    gk_coef = -0.5 * scale_grad * attn_scale * sq_sum / denominator
    dq_rows = attn_scale[None, :, None] * jnp.einsum('nhf,hef->nhe', grad_full, kv_state, precision=lax.Precision.HIGHEST) + 2.0 * gq_coef[None, :, None] * query_full
    dk_rows = jnp.einsum('nhf,hef->nhe', value_full, dm_state, precision=lax.Precision.HIGHEST) + 2.0 * gk_coef[None, :, None] * key_full
    dv_rows = grad_full + jnp.einsum('nhe,hef->nhf', key_full, dm_state, precision=lax.Precision.HIGHEST)
    dqkv = jnp.stack([dq_rows, dk_rows, dv_rows], axis=2).reshape(row_count, 3 * D).astype(jnp.bfloat16)
    start_acc = g_rows.astype(jnp.float32).reshape(TILES, TILE, D)
    grad_groups = g_rows.reshape(N_NODES, TB, TILE, D)
    dy_acc = spread_back(start_acc, adj_groups, tile_ids, grad_groups)
    dy_rows = dy_acc.reshape(row_count, D).astype(jnp.bfloat16)
    grad_qkv = jnp.dot(x_rows.T, dqkv, preferred_element_type=jnp.float32)
    grad_gcn = jnp.dot(x_rows.T, dy_rows, preferred_element_type=jnp.float32)
    gx_rows = (jnp.dot(dqkv, w_qkv.T, preferred_element_type=jnp.float32) + jnp.dot(dy_rows, w_gcn.T, preferred_element_type=jnp.float32)).astype(jnp.bfloat16)
    return (mixed, to_tiles(gx_rows), grad_qkv, grad_gcn)
```

```python
import functools

import jax
import jax.numpy as jnp
from jax import lax
from jax.experimental import pallas as pl
from jax.experimental.pallas import tpu as pltpu
from jax.sharding import PartitionSpec as P

epsilon = 1e-06
HIGHEST = lax.Precision.HIGHEST
SIDE = 8


def contract_rows(left, right):
    return lax.dot_general(
        left, right, (((0,), (0,)), ((), ())), preferred_element_type=jnp.float32
    )


def sum_kernel(
    x_ref, o_ref, core_buf, half_buf, y_buf, piece_buf, z_buf, total, send_core, recv_core,
    send_y, recv_y, send_z, recv_z, send_g, recv_g, send_last, recv_last,
):
    rows = x_ref.shape[0]
    half = rows // 2
    piece = half // SIDE
    me = lax.axis_index("nodes")
    core = lax.rem(me, 2)
    z = lax.rem(me // 2, SIDE)
    y = me // (2 * SIDE)
    partner = me + 1 - 2 * core

    def at_y(k):
        other = lax.rem(y + k, SIDE)
        return other, (other * SIDE + z) * 2 + core

    def at_z(k):
        other = lax.rem(z + k, SIDE)
        return other, (y * SIDE + other) * 2 + core

    barrier = pltpu.get_barrier_semaphore()
    pl.semaphore_signal(barrier, inc=1, device_id={"nodes": partner})
    for k in range(1, SIDE):
        pl.semaphore_signal(barrier, inc=1, device_id={"nodes": at_y(k)[1]})
        pl.semaphore_signal(barrier, inc=1, device_id={"nodes": at_z(k)[1]})
    pl.semaphore_wait(barrier, 2 * SIDE - 1)

    def block(start, size):
        return pl.ds(pl.multiple_of(start, 8), size)

    copies = []

    def send(src, dst, send_sem, recv_sem, target):
        copy = pltpu.make_async_remote_copy(
            src_ref=src, dst_ref=dst, send_sem=send_sem, recv_sem=recv_sem,
            device_id={"nodes": target},
        )
        copy.start()
        copies.append(copy)
        return copy

    first = send(
        x_ref.at[block((1 - core) * half, half)], core_buf, send_core, recv_core, partner
    )
    first.wait_recv()
    half_buf[...] = x_ref[block(core * half, half), :] + core_buf[...]

    stage = []
    for k in range(1, SIDE):
        other, target = at_y(k)
        stage.append(
            send(
                half_buf.at[block(other * piece, piece)], y_buf.at[y],
                send_y.at[k - 1], recv_y.at[k - 1], target,
            )
        )
    y_buf[y] = half_buf[block(y * piece, piece), :]
    for copy in stage:
        copy.wait_recv()
    acc = y_buf[0]
    for k in range(1, SIDE):
        acc = acc + y_buf[k]
    piece_buf[...] = acc

    stage = []
    for k in range(1, SIDE):
        other, target = at_z(k)
        stage.append(
            send(piece_buf, z_buf.at[z], send_z.at[k - 1], recv_z.at[k - 1], target)
        )
    z_buf[z] = acc
    for copy in stage:
        copy.wait_recv()
    acc = z_buf[0]
    for k in range(1, SIDE):
        acc = acc + z_buf[k]
    mine = block(core * half + y * piece, piece)
    total[mine, :] = acc

    stage = []
    for k in range(1, SIDE):
        other, target = at_y(k)
        stage.append(
            send(total.at[mine], total.at[mine], send_g.at[k - 1], recv_g.at[k - 1], target)
        )
    for copy in stage:
        copy.wait_recv()

    whole = block(core * half, half)
    last = send(total.at[whole], total.at[whole], send_last, recv_last, partner)
    last.wait_recv()
    for copy in copies:
        copy.wait_send()
    o_ref[...] = total[...]


def sum_nodes(x, collective_id):
    rows, lanes = x.shape
    half = rows // 2
    piece = half // SIDE
    f32 = jnp.float32
    dma = pltpu.SemaphoreType.DMA
    return pl.pallas_call(
        sum_kernel,
        out_shape=jax.ShapeDtypeStruct((rows, lanes), f32),
        in_specs=[pl.BlockSpec(memory_space=pltpu.VMEM)],
        out_specs=pl.BlockSpec(memory_space=pltpu.VMEM),
        scratch_shapes=[
            pltpu.VMEM((half, lanes), f32),
            pltpu.VMEM((half, lanes), f32),
            pltpu.VMEM((SIDE, piece, lanes), f32),
            pltpu.VMEM((piece, lanes), f32),
            pltpu.VMEM((SIDE, piece, lanes), f32),
            pltpu.VMEM((rows, lanes), f32),
            dma, dma,
            dma((SIDE - 1,)), dma((SIDE - 1,)),
            dma((SIDE - 1,)), dma((SIDE - 1,)),
            dma((SIDE - 1,)), dma((SIDE - 1,)),
            dma, dma,
        ],
        compiler_params=pltpu.CompilerParams(
            collective_id=collective_id, has_side_effects=True
        ),
        name="sum_nodes",
    )(x)


def local(feats, w_qkv, w_gcn, nbr_owner, nbr_tile, adj_blocks, grad_out):
    tile_count = nbr_owner.shape[0]
    list_width = nbr_owner.shape[1]
    head_width = w_gcn.shape[1]
    tile_rows_n = feats.shape[2] // head_width
    row_count = tile_count * tile_rows_n
    gathered = lax.all_gather(feats, "feat", axis=1, tiled=True)
    head_count = gathered.shape[1]
    full_rows = (
        gathered.reshape(tile_count, head_count, tile_rows_n, head_width)
        .transpose(0, 2, 1, 3)
        .reshape(row_count, head_count * head_width)
    )
    adj_all = lax.all_gather(adj_blocks, "feat", axis=1, tiled=True)
    grad_rows = grad_out.reshape(row_count, head_width)
    node_count = lax.axis_size("nodes")
    slot_cap = max(2, (tile_count * list_width + node_count - 1) // node_count)
    total_rows = jnp.float32(row_count * node_count)

    owners = nbr_owner.reshape(-1)
    local_ids = nbr_tile.reshape(-1)
    owner_hot = (owners[:, None] == jnp.arange(node_count, dtype=jnp.int32)[None, :]).astype(
        jnp.int32
    )
    rank_within = jnp.sum((jnp.cumsum(owner_hot, axis=0) - owner_hot) * owner_hot, axis=1)
    slot_index = owners * slot_cap + rank_within
    request = jnp.zeros((node_count * slot_cap,), jnp.int32).at[slot_index].set(local_ids)
    incoming = lax.all_to_all(
        request.reshape(node_count, slot_cap), "nodes", split_axis=0, concat_axis=0, tiled=True
    )
    incoming_flat = incoming.reshape(-1)

    grad_tiles = grad_rows.reshape(tile_count, tile_rows_n, head_width)
    back_term = jnp.einsum(
        "tnab,tah->tnbh", adj_all, grad_tiles, preferred_element_type=jnp.float32
    ).astype(jnp.bfloat16)
    outgoing = jnp.zeros((node_count * slot_cap, tile_rows_n * head_width), jnp.bfloat16)
    outgoing = outgoing.at[slot_index].set(
        back_term.reshape(tile_count * list_width, tile_rows_n * head_width)
    )
    returned = lax.all_to_all(
        outgoing.reshape(node_count, slot_cap, tile_rows_n * head_width),
        "nodes",
        split_axis=0,
        concat_axis=0,
        tiled=True,
    )

    proj = jnp.dot(full_rows, w_qkv, preferred_element_type=jnp.float32).astype(jnp.bfloat16)
    query_rows = proj[:, :head_width]
    key_rows = proj[:, head_width : 2 * head_width]
    value_rows = proj[:, 2 * head_width :]
    query_full = query_rows.astype(jnp.float32)
    key_full = key_rows.astype(jnp.float32)
    value_full = value_rows.astype(jnp.float32)
    grad_full = grad_rows.astype(jnp.float32)
    sq_local = jnp.sum(query_full * query_full)
    sk_local = jnp.sum(key_full * key_full)
    kv_local = contract_rows(key_rows, value_rows)
    pq_local = contract_rows(query_rows, grad_rows)
    stacked = jnp.concatenate([proj, grad_rows], axis=1)
    x_local = contract_rows(full_rows, stacked)
    depth = x_local.shape[0]
    lanes = 2 * head_width
    squares = jnp.concatenate(
        [
            jnp.broadcast_to(sq_local, (head_width // 2, lanes)),
            jnp.broadcast_to(sk_local, (head_width // 2, lanes)),
        ],
        axis=0,
    )
    sent = jnp.concatenate(
        [
            x_local[:, :lanes],
            x_local[:, lanes:],
            jnp.concatenate([kv_local, pq_local], axis=1),
            squares,
        ],
        axis=0,
    )
    summed = sum_nodes(sent, 0)
    x_query = summed[:depth, :head_width]
    x_key = summed[:depth, head_width:]
    x_value = summed[depth : 2 * depth, :head_width]
    x_grad = summed[depth : 2 * depth, head_width:]
    kv_state = summed[2 * depth : 2 * depth + head_width, :head_width]
    pq_state = summed[2 * depth : 2 * depth + head_width, head_width:]
    sq_sum = summed[2 * depth + head_width, 0]
    sk_sum = summed[2 * depth + head_width + head_width // 2, 0]
    scale_grad = jnp.sum(pq_state * kv_state)
    attn_scale = jnp.sqrt(total_rows) / jnp.sqrt(sq_sum * sk_sum + epsilon)
    dm_state = attn_scale * pq_state
    denominator = sq_sum * sk_sum + epsilon
    gq_coef = -0.5 * scale_grad * attn_scale * sk_sum / denominator
    gk_coef = -0.5 * scale_grad * attn_scale * sq_sum / denominator
    grad_qkv = jnp.concatenate(
        [
            attn_scale * jnp.dot(x_grad, kv_state.T, precision=HIGHEST)
            + 2.0 * gq_coef * x_query,
            jnp.dot(x_value, dm_state.T, precision=HIGHEST) + 2.0 * gk_coef * x_key,
            x_grad + jnp.dot(x_key, dm_state, precision=HIGHEST),
        ],
        axis=1,
    )

    y_rows = jnp.dot(full_rows, w_gcn, preferred_element_type=jnp.float32).astype(jnp.bfloat16)
    y_tiles = y_rows.reshape(tile_count, tile_rows_n * head_width)
    picked = (
        y_tiles.at[incoming_flat]
        .get(mode="promise_in_bounds")
        .reshape(node_count, slot_cap, tile_rows_n * head_width)
    )
    fetched = lax.all_to_all(picked, "nodes", split_axis=0, concat_axis=0, tiled=True)
    neighbours = (
        fetched.reshape(node_count * slot_cap, tile_rows_n * head_width)
        .at[slot_index]
        .get(mode="promise_in_bounds")
    )
    neighbours = neighbours.reshape(tile_count, list_width, tile_rows_n, head_width)
    gcn_sum = jnp.einsum(
        "tnab,tnbh->tah", adj_all, neighbours, preferred_element_type=jnp.float32
    ).reshape(row_count, head_width)
    mix_rows = jnp.dot(query_full, kv_state, precision=HIGHEST)
    mixed = (value_full + attn_scale * mix_rows + y_rows.astype(jnp.float32) + gcn_sum).astype(
        jnp.bfloat16
    )
    dq_rows = (
        attn_scale * jnp.dot(grad_full, kv_state.T, precision=HIGHEST)
        + 2.0 * gq_coef * query_full
    )
    dk_rows = jnp.dot(value_full, dm_state.T, precision=HIGHEST) + 2.0 * gk_coef * key_full
    dv_rows = grad_full + jnp.dot(key_full, dm_state, precision=HIGHEST)
    dqkv = jnp.concatenate([dq_rows, dk_rows, dv_rows], axis=1).astype(jnp.bfloat16)

    tile_hot = (incoming_flat[:, None] == jnp.arange(tile_count, dtype=jnp.int32)[None, :]).astype(
        jnp.bfloat16
    )
    back_sum = contract_rows(
        tile_hot, returned.reshape(node_count * slot_cap, tile_rows_n * head_width)
    )
    dy_rows = (grad_full + back_sum.reshape(row_count, head_width)).astype(jnp.bfloat16)
    gcn_local = contract_rows(full_rows, dy_rows)
    gcn_sent = jnp.concatenate([gcn_local[: depth // 2], gcn_local[depth // 2 :]], axis=1)
    gcn_summed = sum_nodes(gcn_sent, 1)
    grad_gcn = jnp.concatenate([gcn_summed[:, :head_width], gcn_summed[:, head_width:]], axis=0)
    partial_grad = lax.dot_general(
        dqkv, w_qkv, (((1,), (1,)), ((), ())), preferred_element_type=jnp.float32
    )
    partial_grad = partial_grad + lax.dot_general(
        dy_rows, w_gcn, (((1,), (1,)), ((), ())), preferred_element_type=jnp.float32
    )
    grad_x = lax.psum_scatter(
        partial_grad.astype(jnp.bfloat16), "feat", scatter_dimension=1, tiled=True
    )
    mixed_tiles = mixed.reshape(tile_count, 1, tile_rows_n * head_width)
    grad_x_tiles = grad_x.reshape(tile_count, 1, tile_rows_n * head_width)
    return (mixed_tiles, grad_x_tiles, grad_qkv, grad_gcn)


def solution(mesh):
    in_specs = (
        P("nodes", "feat", None),
        P(None, "feat"),
        P(None, "feat"),
        P("nodes", None),
        P("nodes", None),
        P("nodes", "feat", None, None),
        P("nodes", "feat", None),
    )
    out_specs = (
        P("nodes", "feat", None),
        P("nodes", "feat", None),
        P(None, "feat"),
        P(None, "feat"),
    )
    return jax.shard_map(local, mesh=mesh, in_specs=in_specs, out_specs=out_specs, check_vma=False)
```

```python
import jax
import jax.numpy as jnp
from jax import lax
from jax.experimental import pallas as pl
from jax.experimental.pallas import tpu as pltpu
from jax.sharding import PartitionSpec as P

epsilon = 1e-06
HIGHEST = lax.Precision.HIGHEST
SIDE = 8
CAP = 2
SUM_BYTES = 100_000_000


def contract_rows(left, right):
    return lax.dot_general(
        left, right, (((0,), (0,)), ((), ())), preferred_element_type=jnp.float32
    )


def sum_kernel(
    x_ref, o_ref, core_buf, half_buf, y_buf, piece_buf, z_buf, total, send_core, recv_core,
    send_y, recv_y, send_z, recv_z, send_g, recv_g, send_last, recv_last,
):
    rows = x_ref.shape[0]
    half = rows // 2
    piece = half // SIDE
    me = lax.axis_index("nodes")
    core = lax.rem(me, 2)
    z = lax.rem(me // 2, SIDE)
    y = me // (2 * SIDE)
    partner = me + 1 - 2 * core

    def at_y(k):
        other = lax.rem(y + k, SIDE)
        return other, (other * SIDE + z) * 2 + core

    def at_z(k):
        other = lax.rem(z + k, SIDE)
        return other, (y * SIDE + other) * 2 + core

    barrier = pltpu.get_barrier_semaphore()
    pl.semaphore_signal(barrier, inc=1, device_id={"nodes": partner})
    for k in range(1, SIDE):
        pl.semaphore_signal(barrier, inc=1, device_id={"nodes": at_y(k)[1]})
        pl.semaphore_signal(barrier, inc=1, device_id={"nodes": at_z(k)[1]})
    pl.semaphore_wait(barrier, 2 * SIDE - 1)

    def block(start, size):
        return pl.ds(pl.multiple_of(start, 8), size)

    copies = []

    def send(src, dst, send_sem, recv_sem, target):
        copy = pltpu.make_async_remote_copy(
            src_ref=src, dst_ref=dst, send_sem=send_sem, recv_sem=recv_sem,
            device_id={"nodes": target},
        )
        copy.start()
        copies.append(copy)
        return copy

    first = send(
        x_ref.at[block((1 - core) * half, half)], core_buf, send_core, recv_core, partner
    )
    first.wait_recv()
    half_buf[...] = x_ref[block(core * half, half), :] + core_buf[...]

    stage = []
    for k in range(1, SIDE):
        other, target = at_y(k)
        stage.append(
            send(
                half_buf.at[block(other * piece, piece)], y_buf.at[y],
                send_y.at[k - 1], recv_y.at[k - 1], target,
            )
        )
    y_buf[y] = half_buf[block(y * piece, piece), :]
    for copy in stage:
        copy.wait_recv()
    acc = y_buf[0]
    for k in range(1, SIDE):
        acc = acc + y_buf[k]
    piece_buf[...] = acc

    stage = []
    for k in range(1, SIDE):
        other, target = at_z(k)
        stage.append(
            send(piece_buf, z_buf.at[z], send_z.at[k - 1], recv_z.at[k - 1], target)
        )
    z_buf[z] = acc
    for copy in stage:
        copy.wait_recv()
    acc = z_buf[0]
    for k in range(1, SIDE):
        acc = acc + z_buf[k]
    mine = block(core * half + y * piece, piece)
    total[mine, :] = acc

    stage = []
    for k in range(1, SIDE):
        other, target = at_y(k)
        stage.append(
            send(total.at[mine], total.at[mine], send_g.at[k - 1], recv_g.at[k - 1], target)
        )
    for copy in stage:
        copy.wait_recv()

    whole = block(core * half, half)
    last = send(total.at[whole], total.at[whole], send_last, recv_last, partner)
    last.wait_recv()
    for copy in copies:
        copy.wait_send()
    o_ref[...] = total[...]


def sum_nodes(x, collective_id):
    rows, lanes = x.shape
    half = rows // 2
    piece = half // SIDE
    f32 = jnp.float32
    dma = pltpu.SemaphoreType.DMA
    return pl.pallas_call(
        sum_kernel,
        out_shape=jax.ShapeDtypeStruct((rows, lanes), f32),
        in_specs=[pl.BlockSpec(memory_space=pltpu.VMEM)],
        out_specs=pl.BlockSpec(memory_space=pltpu.VMEM),
        scratch_shapes=[
            pltpu.VMEM((half, lanes), f32),
            pltpu.VMEM((half, lanes), f32),
            pltpu.VMEM((SIDE, piece, lanes), f32),
            pltpu.VMEM((piece, lanes), f32),
            pltpu.VMEM((SIDE, piece, lanes), f32),
            pltpu.VMEM((rows, lanes), f32),
            dma, dma,
            dma((SIDE - 1,)), dma((SIDE - 1,)),
            dma((SIDE - 1,)), dma((SIDE - 1,)),
            dma((SIDE - 1,)), dma((SIDE - 1,)),
            dma, dma,
        ],
        compiler_params=pltpu.CompilerParams(
            collective_id=collective_id, has_side_effects=True
        ),
        cost_estimate=pl.CostEstimate(
            flops=0, bytes_accessed=SUM_BYTES, transcendentals=0
        ),
        name="sum_nodes",
    )(x)


def pack(tile):
    half = tile.shape[0] // 2
    return jnp.concatenate([tile[:half], tile[half:]], axis=1)


def unpack(tile):
    half = tile.shape[1] // 2
    return jnp.concatenate([tile[:, :half], tile[:, half:]], axis=0)


def back_kernel(slot_ref, adj_ref, grad_ref, out_ref, terms, sem):
    tiles, width = adj_ref.shape[0], adj_ref.shape[1]

    def one_tile(t, carry):
        grad = grad_ref[t]
        for n in range(width):
            term = lax.dot_general(
                adj_ref[t, n], grad, (((0,), (0,)), ((), ())),
                preferred_element_type=jnp.float32,
            )
            j = t * width + n
            terms[j] = pack(term).astype(jnp.bfloat16)
        return carry

    lax.fori_loop(0, tiles, one_tile, 0)

    def place(j, carry):
        pltpu.make_async_copy(terms.at[j], out_ref.at[slot_ref[j]], sem).start()
        return carry

    lax.fori_loop(0, tiles * width, place, 0)
    pltpu.make_async_copy(terms, out_ref.at[pl.ds(0, tiles * width)], sem).wait()


def place_back_terms(slot_index, adj_all, grad_tiles, slots):
    tiles, width = adj_all.shape[:2]
    rows, columns = grad_tiles.shape[1:]
    packed = (rows // 2, columns * 2)
    return pl.pallas_call(
        back_kernel,
        out_shape=jax.ShapeDtypeStruct((slots,) + packed, jnp.bfloat16),
        in_specs=[
            pl.BlockSpec(memory_space=pltpu.SMEM),
            pl.BlockSpec(memory_space=pltpu.VMEM),
            pl.BlockSpec(memory_space=pltpu.VMEM),
        ],
        out_specs=pl.BlockSpec(memory_space=pl.ANY),
        scratch_shapes=[
            pltpu.VMEM((tiles * width,) + packed, jnp.bfloat16),
            pltpu.SemaphoreType.DMA,
        ],
        name="place_back_terms",
    )(slot_index, adj_all, grad_tiles)


def pick_kernel(id_ref, y_ref, out_ref, packed_ref, sem):
    for t in range(y_ref.shape[0]):
        packed_ref[t] = pack(y_ref[t].astype(jnp.float32)).astype(jnp.bfloat16)

    def place(j, carry):
        pltpu.make_async_copy(packed_ref.at[id_ref[j]], out_ref.at[j], sem).start()
        return carry

    lax.fori_loop(0, out_ref.shape[0], place, 0)
    pltpu.make_async_copy(out_ref, out_ref, sem).wait()


def pick_tiles(ids, y_tiles):
    tiles, rows, columns = y_tiles.shape
    packed = (rows // 2, columns * 2)
    return pl.pallas_call(
        pick_kernel,
        out_shape=jax.ShapeDtypeStruct((ids.shape[0],) + packed, jnp.bfloat16),
        in_specs=[
            pl.BlockSpec(memory_space=pltpu.SMEM),
            pl.BlockSpec(memory_space=pltpu.VMEM),
        ],
        out_specs=pl.BlockSpec(memory_space=pl.ANY),
        scratch_shapes=[
            pltpu.VMEM((tiles,) + packed, jnp.bfloat16),
            pltpu.SemaphoreType.DMA,
        ],
        name="pick_tiles",
    )(ids, y_tiles)


def add_kernel(id_ref, returned_ref, grad_ref, dy_ref, acc):
    acc[...] = jnp.zeros_like(acc)

    def add(j, carry):
        tile = id_ref[j]

        @pl.when(tile >= 0)
        def _():
            acc[tile] = acc[tile] + returned_ref[j].astype(jnp.float32)

        return carry

    lax.fori_loop(0, returned_ref.shape[0], add, 0)
    for t in range(grad_ref.shape[0]):
        total = grad_ref[t].astype(jnp.float32) + unpack(acc[t])
        dy_ref[t] = total.astype(jnp.bfloat16)


def add_returned(ids, returned, grad_tiles):
    tiles, rows, columns = grad_tiles.shape
    return pl.pallas_call(
        add_kernel,
        out_shape=jax.ShapeDtypeStruct(grad_tiles.shape, jnp.bfloat16),
        in_specs=[
            pl.BlockSpec(memory_space=pltpu.SMEM),
            pl.BlockSpec(memory_space=pltpu.VMEM),
            pl.BlockSpec(memory_space=pltpu.VMEM),
        ],
        out_specs=pl.BlockSpec(memory_space=pltpu.VMEM),
        scratch_shapes=[pltpu.VMEM((tiles, rows // 2, columns * 2), jnp.float32)],
        name="add_returned",
    )(ids, returned, grad_tiles)


def mixed_kernel(slot_ref, fetched_ref, adj_ref, base_ref, out_ref, held, sem):
    tiles, width = adj_ref.shape[0], adj_ref.shape[1]

    def fetch(j, carry):
        pltpu.make_async_copy(fetched_ref.at[slot_ref[j]], held.at[j], sem).start()
        return carry

    lax.fori_loop(0, tiles * width, fetch, 0)
    pltpu.make_async_copy(fetched_ref.at[pl.ds(0, tiles * width)], held, sem).wait()

    def one_tile(t, carry):
        acc = base_ref[t]
        for n in range(width):
            rows = unpack(held[t * width + n].astype(jnp.float32)).astype(jnp.bfloat16)
            acc = acc + jnp.dot(adj_ref[t, n], rows, preferred_element_type=jnp.float32)
        out_ref[t] = acc.astype(jnp.bfloat16)
        return carry

    lax.fori_loop(0, tiles, one_tile, 0)


def finish_mixed(slot_index, fetched, adj_all, base):
    tiles, width = adj_all.shape[:2]
    return pl.pallas_call(
        mixed_kernel,
        out_shape=jax.ShapeDtypeStruct(base.shape, jnp.bfloat16),
        in_specs=[
            pl.BlockSpec(memory_space=pltpu.SMEM),
            pl.BlockSpec(memory_space=pl.ANY),
            pl.BlockSpec(memory_space=pltpu.VMEM),
            pl.BlockSpec(memory_space=pltpu.VMEM),
        ],
        out_specs=pl.BlockSpec(memory_space=pltpu.VMEM),
        scratch_shapes=[
            pltpu.VMEM((tiles * width,) + fetched.shape[1:], jnp.bfloat16),
            pltpu.SemaphoreType.DMA,
        ],
        name="finish_mixed",
    )(slot_index, fetched, adj_all, base)


def local(feats, w_qkv, w_gcn, nbr_owner, nbr_tile, adj_blocks, grad_out):
    tile_count = nbr_owner.shape[0]
    list_width = nbr_owner.shape[1]
    head_width = w_gcn.shape[1]
    tile_rows_n = feats.shape[2] // head_width
    row_count = tile_count * tile_rows_n
    node_count = lax.axis_size("nodes")
    slots = node_count * CAP
    entries = tile_count * list_width
    total_rows = jnp.float32(row_count * node_count)
    adj_all = lax.all_gather(adj_blocks, "feat", axis=1, tiled=True)
    gathered = lax.all_gather(feats, "feat", axis=1, tiled=True)
    gathered, grad_out = lax.optimization_barrier((gathered, grad_out))
    head_count = gathered.shape[1]
    full_rows = (
        gathered.reshape(tile_count, head_count, tile_rows_n, head_width)
        .transpose(0, 2, 1, 3)
        .reshape(row_count, head_count * head_width)
    )
    grad_tiles = grad_out.reshape(tile_count, tile_rows_n, head_width)
    grad_rows = grad_tiles.reshape(row_count, head_width)

    owners = nbr_owner.reshape(-1)
    place = jnp.arange(entries, dtype=jnp.int32)
    earlier = place[:, None] > place[None, :]
    same = owners[:, None] == owners[None, :]
    rank_within = jnp.sum((earlier & same).astype(jnp.int32), axis=1)
    slot_index = owners * CAP + rank_within

    proj = jnp.dot(full_rows, w_qkv, preferred_element_type=jnp.float32).astype(jnp.bfloat16)
    query_rows = proj[:, :head_width]
    key_rows = proj[:, head_width : 2 * head_width]
    value_rows = proj[:, 2 * head_width :]
    query_full = query_rows.astype(jnp.float32)
    key_full = key_rows.astype(jnp.float32)
    value_full = value_rows.astype(jnp.float32)
    grad_full = grad_rows.astype(jnp.float32)
    sq_local = jnp.sum(query_full * query_full)
    sk_local = jnp.sum(key_full * key_full)
    kv_local = contract_rows(key_rows, value_rows)
    pq_local = contract_rows(query_rows, grad_rows)
    stacked = jnp.concatenate([proj, grad_rows], axis=1)
    x_local = contract_rows(full_rows, stacked)
    depth = x_local.shape[0]
    lanes = 2 * head_width
    squares = jnp.concatenate(
        [
            jnp.broadcast_to(sq_local, (head_width // 2, lanes)),
            jnp.broadcast_to(sk_local, (head_width // 2, lanes)),
        ],
        axis=0,
    )
    codes = jnp.pad(
        (nbr_owner * tile_count + nbr_tile).reshape(-1).astype(jnp.float32),
        (0, lanes - entries),
    )
    own_row = jnp.arange(node_count, dtype=jnp.int32) == lax.axis_index("nodes")
    own_list = jnp.where(own_row[:, None], codes[None, :], 0.0)
    sent = jnp.concatenate(
        [
            x_local[:, :lanes],
            x_local[:, lanes:],
            jnp.concatenate([kv_local, pq_local], axis=1),
            squares,
            own_list,
        ],
        axis=0,
    )
    summed = sum_nodes(sent, 0)
    summed, adj_all = lax.optimization_barrier((summed, adj_all))
    outgoing = place_back_terms(slot_index, adj_all, grad_tiles, slots)
    exchange_shape = (node_count, CAP) + outgoing.shape[1:]
    returned = lax.all_to_all(
        outgoing.reshape(exchange_shape), "nodes", split_axis=0, concat_axis=0, tiled=True
    ).reshape(outgoing.shape)

    listed = summed[2 * depth + lanes :, :entries].astype(jnp.int32)
    wanted = listed // tile_count == lax.axis_index("nodes")
    before = jnp.dot(
        wanted.astype(jnp.bfloat16),
        earlier.T.astype(jnp.bfloat16),
        preferred_element_type=jnp.float32,
    )
    marked = jnp.where(wanted, listed % tile_count + 1, 0)
    incoming = (
        jnp.stack(
            [jnp.sum(jnp.where(before == r, marked, 0), axis=1) for r in range(CAP)], axis=1
        ).reshape(-1)
        - 1
    )

    y_rows = jnp.dot(full_rows, w_gcn, preferred_element_type=jnp.float32).astype(jnp.bfloat16)
    picked = pick_tiles(
        jnp.maximum(incoming, 0), y_rows.reshape(tile_count, tile_rows_n, head_width)
    )
    fetched = lax.all_to_all(
        picked.reshape(exchange_shape), "nodes", split_axis=0, concat_axis=0, tiled=True
    ).reshape(outgoing.shape)
    x_query = summed[:depth, :head_width]
    x_key = summed[:depth, head_width:]
    x_value = summed[depth : 2 * depth, :head_width]
    x_grad = summed[depth : 2 * depth, head_width:]
    kv_state = summed[2 * depth : 2 * depth + head_width, :head_width]
    pq_state = summed[2 * depth : 2 * depth + head_width, head_width:]
    sq_sum = summed[2 * depth + head_width, 0]
    sk_sum = summed[2 * depth + head_width + head_width // 2, 0]
    scale_grad = jnp.sum(pq_state * kv_state)
    attn_scale = jnp.sqrt(total_rows) / jnp.sqrt(sq_sum * sk_sum + epsilon)
    dm_state = attn_scale * pq_state
    denominator = sq_sum * sk_sum + epsilon
    gq_coef = -0.5 * scale_grad * attn_scale * sk_sum / denominator
    gk_coef = -0.5 * scale_grad * attn_scale * sq_sum / denominator
    grad_qkv = jnp.concatenate(
        [
            attn_scale * jnp.dot(x_grad, kv_state.T, precision=HIGHEST)
            + 2.0 * gq_coef * x_query,
            jnp.dot(x_value, dm_state.T, precision=HIGHEST) + 2.0 * gk_coef * x_key,
            x_grad + jnp.dot(x_key, dm_state, precision=HIGHEST),
        ],
        axis=1,
    )

    mix_rows = jnp.dot(query_full, kv_state, precision=HIGHEST)
    base = value_full + attn_scale * mix_rows + y_rows.astype(jnp.float32)
    dq_rows = (
        attn_scale * jnp.dot(grad_full, kv_state.T, precision=HIGHEST)
        + 2.0 * gq_coef * query_full
    )
    dk_rows = jnp.dot(value_full, dm_state.T, precision=HIGHEST) + 2.0 * gk_coef * key_full
    dv_rows = grad_full + jnp.dot(key_full, dm_state, precision=HIGHEST)
    dqkv = jnp.concatenate([dq_rows, dk_rows, dv_rows], axis=1).astype(jnp.bfloat16)

    dy_rows = add_returned(incoming, returned, grad_tiles).reshape(row_count, head_width)
    gcn_local = contract_rows(full_rows, dy_rows)
    gcn_sent = jnp.concatenate([gcn_local[: depth // 2], gcn_local[depth // 2 :]], axis=1)
    gcn_summed = sum_nodes(gcn_sent, 1)
    grad_gcn = jnp.concatenate([gcn_summed[:, :head_width], gcn_summed[:, head_width:]], axis=0)
    partial_grad = lax.dot_general(
        dqkv, w_qkv, (((1,), (1,)), ((), ())), preferred_element_type=jnp.float32
    )
    partial_grad = partial_grad + lax.dot_general(
        dy_rows, w_gcn, (((1,), (1,)), ((), ())), preferred_element_type=jnp.float32
    )
    grad_x = lax.psum_scatter(
        partial_grad.astype(jnp.bfloat16), "feat", scatter_dimension=1, tiled=True
    )
    mixed = finish_mixed(
        slot_index, fetched, adj_all, base.reshape(tile_count, tile_rows_n, head_width)
    )
    mixed_tiles = mixed.reshape(tile_count, 1, tile_rows_n * head_width)
    grad_x_tiles = grad_x.reshape(tile_count, 1, tile_rows_n * head_width)
    return (mixed_tiles, grad_x_tiles, grad_qkv, grad_gcn)


def solution(mesh):
    in_specs = (
        P("nodes", "feat", None),
        P(None, "feat"),
        P(None, "feat"),
        P("nodes", None),
        P("nodes", None),
        P("nodes", "feat", None, None),
        P("nodes", "feat", None),
    )
    out_specs = (
        P("nodes", "feat", None),
        P("nodes", "feat", None),
        P(None, "feat"),
        P(None, "feat"),
    )
    return jax.shard_map(local, mesh=mesh, in_specs=in_specs, out_specs=out_specs, check_vma=False)
```

```python
import jax
import jax.numpy as jnp
from jax import lax
from jax.experimental import pallas as pl
from jax.experimental.pallas import tpu as pltpu
from jax.sharding import PartitionSpec as P

epsilon = 1e-06
HIGHEST = lax.Precision.HIGHEST
SIDE = 8
CAP = 2
SUM_BYTES = 100_000_000


def contract_rows(left, right):
    return lax.dot_general(
        left, right, (((0,), (0,)), ((), ())), preferred_element_type=jnp.float32
    )


def sum_kernel(
    x_ref, o_ref, core_buf, half_buf, y_buf, piece_buf, z_buf, total, send_core, recv_core,
    send_y, recv_y, send_z, recv_z, send_g, recv_g, send_last, recv_last,
):
    rows = x_ref.shape[0]
    half = rows // 2
    piece = half // SIDE
    me = lax.axis_index("nodes")
    core = lax.rem(me, 2)
    z = lax.rem(me // 2, SIDE)
    y = me // (2 * SIDE)
    partner = me + 1 - 2 * core

    def at_y(k):
        other = lax.rem(y + k, SIDE)
        return other, (other * SIDE + z) * 2 + core

    def at_z(k):
        other = lax.rem(z + k, SIDE)
        return other, (y * SIDE + other) * 2 + core

    barrier = pltpu.get_barrier_semaphore()
    pl.semaphore_signal(barrier, inc=1, device_id={"nodes": partner})
    for k in range(1, SIDE):
        pl.semaphore_signal(barrier, inc=1, device_id={"nodes": at_y(k)[1]})
        pl.semaphore_signal(barrier, inc=1, device_id={"nodes": at_z(k)[1]})
    pl.semaphore_wait(barrier, 2 * SIDE - 1)

    def block(start, size):
        return pl.ds(pl.multiple_of(start, 8), size)

    copies = []

    def send(src, dst, send_sem, recv_sem, target):
        copy = pltpu.make_async_remote_copy(
            src_ref=src, dst_ref=dst, send_sem=send_sem, recv_sem=recv_sem,
            device_id={"nodes": target},
        )
        copy.start()
        copies.append(copy)
        return copy

    first = send(
        x_ref.at[block((1 - core) * half, half)], core_buf, send_core, recv_core, partner
    )
    first.wait_recv()
    half_buf[...] = x_ref[block(core * half, half), :] + core_buf[...]

    stage = []
    for k in range(1, SIDE):
        other, target = at_y(k)
        stage.append(
            send(
                half_buf.at[block(other * piece, piece)], y_buf.at[y],
                send_y.at[k - 1], recv_y.at[k - 1], target,
            )
        )
    y_buf[y] = half_buf[block(y * piece, piece), :]
    for copy in stage:
        copy.wait_recv()
    acc = y_buf[0]
    for k in range(1, SIDE):
        acc = acc + y_buf[k]
    piece_buf[...] = acc

    stage = []
    for k in range(1, SIDE):
        other, target = at_z(k)
        stage.append(
            send(piece_buf, z_buf.at[z], send_z.at[k - 1], recv_z.at[k - 1], target)
        )
    z_buf[z] = acc
    for copy in stage:
        copy.wait_recv()
    acc = z_buf[0]
    for k in range(1, SIDE):
        acc = acc + z_buf[k]
    mine = block(core * half + y * piece, piece)
    total[mine, :] = acc

    stage = []
    for k in range(1, SIDE):
        other, target = at_y(k)
        stage.append(
            send(total.at[mine], total.at[mine], send_g.at[k - 1], recv_g.at[k - 1], target)
        )
    for copy in stage:
        copy.wait_recv()

    whole = block(core * half, half)
    last = send(total.at[whole], total.at[whole], send_last, recv_last, partner)
    last.wait_recv()
    for copy in copies:
        copy.wait_send()
    o_ref[...] = total[...]


def sum_nodes(x, collective_id):
    rows, lanes = x.shape
    half = rows // 2
    piece = half // SIDE
    f32 = jnp.float32
    dma = pltpu.SemaphoreType.DMA
    return pl.pallas_call(
        sum_kernel,
        out_shape=jax.ShapeDtypeStruct((rows, lanes), f32),
        in_specs=[pl.BlockSpec(memory_space=pltpu.VMEM)],
        out_specs=pl.BlockSpec(memory_space=pltpu.VMEM),
        scratch_shapes=[
            pltpu.VMEM((half, lanes), f32),
            pltpu.VMEM((half, lanes), f32),
            pltpu.VMEM((SIDE, piece, lanes), f32),
            pltpu.VMEM((piece, lanes), f32),
            pltpu.VMEM((SIDE, piece, lanes), f32),
            pltpu.VMEM((rows, lanes), f32),
            dma, dma,
            dma((SIDE - 1,)), dma((SIDE - 1,)),
            dma((SIDE - 1,)), dma((SIDE - 1,)),
            dma((SIDE - 1,)), dma((SIDE - 1,)),
            dma, dma,
        ],
        compiler_params=pltpu.CompilerParams(
            collective_id=collective_id, has_side_effects=True
        ),
        cost_estimate=pl.CostEstimate(
            flops=0, bytes_accessed=SUM_BYTES, transcendentals=0
        ),
        name="sum_nodes",
    )(x)


def pack(tile):
    half = tile.shape[0] // 2
    return jnp.concatenate([tile[:half], tile[half:]], axis=1)


def unpack(tile):
    half = tile.shape[1] // 2
    return jnp.concatenate([tile[:, :half], tile[:, half:]], axis=0)


def back_kernel(slot_ref, adj_ref, grad_ref, out_ref, terms, sem):
    tiles, width = adj_ref.shape[0], adj_ref.shape[1]

    def one_tile(t, carry):
        grad = grad_ref[t]
        for n in range(width):
            term = lax.dot_general(
                adj_ref[t, n], grad, (((0,), (0,)), ((), ())),
                preferred_element_type=jnp.float32,
            )
            j = t * width + n
            terms[j] = pack(term).astype(jnp.bfloat16)
        return carry

    lax.fori_loop(0, tiles, one_tile, 0, unroll=4)

    def place(j, carry):
        pltpu.make_async_copy(terms.at[j], out_ref.at[slot_ref[j]], sem).start()
        return carry

    lax.fori_loop(0, tiles * width, place, 0)
    pltpu.make_async_copy(terms, out_ref.at[pl.ds(0, tiles * width)], sem).wait()


def place_back_terms(slot_index, adj_all, grad_tiles, slots):
    tiles, width = adj_all.shape[:2]
    rows, columns = grad_tiles.shape[1:]
    packed = (rows // 2, columns * 2)
    return pl.pallas_call(
        back_kernel,
        out_shape=jax.ShapeDtypeStruct((slots,) + packed, jnp.bfloat16),
        in_specs=[
            pl.BlockSpec(memory_space=pltpu.SMEM),
            pl.BlockSpec(memory_space=pltpu.VMEM),
            pl.BlockSpec(memory_space=pltpu.VMEM),
        ],
        out_specs=pl.BlockSpec(memory_space=pl.ANY),
        scratch_shapes=[
            pltpu.VMEM((tiles * width,) + packed, jnp.bfloat16),
            pltpu.SemaphoreType.DMA,
        ],
        name="place_back_terms",
    )(slot_index, adj_all, grad_tiles)


def pick_kernel(id_ref, y_ref, out_ref, packed_ref, sem):
    for t in range(y_ref.shape[0]):
        packed_ref[t] = pack(y_ref[t].astype(jnp.float32)).astype(jnp.bfloat16)

    def place(j, carry):
        pltpu.make_async_copy(packed_ref.at[id_ref[j]], out_ref.at[j], sem).start()
        return carry

    lax.fori_loop(0, out_ref.shape[0], place, 0)
    pltpu.make_async_copy(out_ref, out_ref, sem).wait()


def pick_tiles(ids, y_tiles):
    tiles, rows, columns = y_tiles.shape
    packed = (rows // 2, columns * 2)
    return pl.pallas_call(
        pick_kernel,
        out_shape=jax.ShapeDtypeStruct((ids.shape[0],) + packed, jnp.bfloat16),
        in_specs=[
            pl.BlockSpec(memory_space=pltpu.SMEM),
            pl.BlockSpec(memory_space=pltpu.VMEM),
        ],
        out_specs=pl.BlockSpec(memory_space=pl.ANY),
        scratch_shapes=[
            pltpu.VMEM((tiles,) + packed, jnp.bfloat16),
            pltpu.SemaphoreType.DMA,
        ],
        name="pick_tiles",
    )(ids, y_tiles)


def add_kernel(id_ref, returned_ref, grad_ref, dy_ref, acc):
    acc[...] = jnp.zeros_like(acc)

    def add(j, carry):
        tile = id_ref[j]

        @pl.when(tile >= 0)
        def _():
            acc[tile] = acc[tile] + returned_ref[j].astype(jnp.float32)

        return carry

    lax.fori_loop(0, returned_ref.shape[0], add, 0)
    for t in range(grad_ref.shape[0]):
        total = grad_ref[t].astype(jnp.float32) + unpack(acc[t])
        dy_ref[t] = total.astype(jnp.bfloat16)


def add_returned(ids, returned, grad_tiles):
    tiles, rows, columns = grad_tiles.shape
    return pl.pallas_call(
        add_kernel,
        out_shape=jax.ShapeDtypeStruct(grad_tiles.shape, jnp.bfloat16),
        in_specs=[
            pl.BlockSpec(memory_space=pltpu.SMEM),
            pl.BlockSpec(memory_space=pltpu.VMEM),
            pl.BlockSpec(memory_space=pltpu.VMEM),
        ],
        out_specs=pl.BlockSpec(memory_space=pltpu.VMEM),
        scratch_shapes=[pltpu.VMEM((tiles, rows // 2, columns * 2), jnp.float32)],
        name="add_returned",
    )(ids, returned, grad_tiles)


def mixed_kernel(slot_ref, fetched_ref, adj_ref, base_ref, out_ref, held, sem):
    tiles, width = adj_ref.shape[0], adj_ref.shape[1]

    def fetch(j, carry):
        pltpu.make_async_copy(fetched_ref.at[slot_ref[j]], held.at[j], sem).start()
        return carry

    lax.fori_loop(0, tiles * width, fetch, 0)
    pltpu.make_async_copy(fetched_ref.at[pl.ds(0, tiles * width)], held, sem).wait()

    def one_tile(t, carry):
        acc = base_ref[t]
        for n in range(width):
            rows = unpack(held[t * width + n].astype(jnp.float32)).astype(jnp.bfloat16)
            acc = acc + jnp.dot(adj_ref[t, n], rows, preferred_element_type=jnp.float32)
        out_ref[t] = acc.astype(jnp.bfloat16)
        return carry

    lax.fori_loop(0, tiles, one_tile, 0, unroll=4)


def finish_mixed(slot_index, fetched, adj_all, base):
    tiles, width = adj_all.shape[:2]
    return pl.pallas_call(
        mixed_kernel,
        out_shape=jax.ShapeDtypeStruct(base.shape, jnp.bfloat16),
        in_specs=[
            pl.BlockSpec(memory_space=pltpu.SMEM),
            pl.BlockSpec(memory_space=pl.ANY),
            pl.BlockSpec(memory_space=pltpu.VMEM),
            pl.BlockSpec(memory_space=pltpu.VMEM),
        ],
        out_specs=pl.BlockSpec(memory_space=pltpu.VMEM),
        scratch_shapes=[
            pltpu.VMEM((tiles * width,) + fetched.shape[1:], jnp.bfloat16),
            pltpu.SemaphoreType.DMA,
        ],
        name="finish_mixed",
    )(slot_index, fetched, adj_all, base)


def local(feats, w_qkv, w_gcn, nbr_owner, nbr_tile, adj_blocks, grad_out):
    tile_count = nbr_owner.shape[0]
    list_width = nbr_owner.shape[1]
    head_width = w_gcn.shape[1]
    tile_rows_n = feats.shape[2] // head_width
    row_count = tile_count * tile_rows_n
    node_count = lax.axis_size("nodes")
    slots = node_count * CAP
    entries = tile_count * list_width
    total_rows = jnp.float32(row_count * node_count)
    adj_all = lax.all_gather(adj_blocks, "feat", axis=1, tiled=True)
    gathered = lax.all_gather(feats, "feat", axis=1, tiled=True)
    gathered, grad_out = lax.optimization_barrier((gathered, grad_out))
    head_count = gathered.shape[1]
    full_rows = (
        gathered.reshape(tile_count, head_count, tile_rows_n, head_width)
        .transpose(0, 2, 1, 3)
        .reshape(row_count, head_count * head_width)
    )
    grad_tiles = grad_out.reshape(tile_count, tile_rows_n, head_width)
    grad_rows = grad_tiles.reshape(row_count, head_width)

    owners = nbr_owner.reshape(-1)
    place = jnp.arange(entries, dtype=jnp.int32)
    earlier = place[:, None] > place[None, :]
    same = owners[:, None] == owners[None, :]
    rank_within = jnp.sum((earlier & same).astype(jnp.int32), axis=1)
    slot_index = owners * CAP + rank_within

    proj = jnp.dot(full_rows, w_qkv, preferred_element_type=jnp.float32).astype(jnp.bfloat16)
    query_rows = proj[:, :head_width]
    key_rows = proj[:, head_width : 2 * head_width]
    value_rows = proj[:, 2 * head_width :]
    query_full = query_rows.astype(jnp.float32)
    key_full = key_rows.astype(jnp.float32)
    value_full = value_rows.astype(jnp.float32)
    grad_full = grad_rows.astype(jnp.float32)
    sq_local = jnp.sum(query_full * query_full)
    sk_local = jnp.sum(key_full * key_full)
    kv_local = contract_rows(key_rows, value_rows)
    pq_local = contract_rows(query_rows, grad_rows)
    stacked = jnp.concatenate([proj, grad_rows], axis=1)
    x_local = contract_rows(full_rows, stacked)
    depth = x_local.shape[0]
    lanes = 2 * head_width
    me = lax.axis_index("nodes")
    codes = jnp.pad(
        (nbr_owner * tile_count + nbr_tile).reshape(-1).astype(jnp.float32),
        (0, head_width - entries),
    )
    list_row = lax.broadcasted_iota(jnp.int32, (node_count // 2, lanes), 0)
    list_lane = lax.broadcasted_iota(jnp.int32, (node_count // 2, lanes), 1)
    mine = (list_row == me // 2) & (list_lane // head_width == me % 2)
    own_list = jnp.where(mine, jnp.tile(codes, 2)[None, :], 0.0)
    first = list_row == 0
    own_list = own_list + jnp.where(first & (list_lane == entries), sq_local, 0.0)
    own_list = own_list + jnp.where(first & (list_lane == entries + 1), sk_local, 0.0)
    sent = jnp.concatenate(
        [
            x_local[:, :lanes],
            x_local[:, lanes:],
            jnp.concatenate([kv_local, pq_local], axis=1),
            own_list,
        ],
        axis=0,
    )
    summed = sum_nodes(sent, 0)
    summed, adj_all = lax.optimization_barrier((summed, adj_all))
    outgoing = place_back_terms(slot_index, adj_all, grad_tiles, slots)
    exchange_shape = (node_count, CAP) + outgoing.shape[1:]
    returned = lax.all_to_all(
        outgoing.reshape(exchange_shape), "nodes", split_axis=0, concat_axis=0, tiled=True
    ).reshape(outgoing.shape)

    lists = summed[2 * depth + head_width :]
    listed = (
        jnp.stack([lists[:, :entries], lists[:, head_width : head_width + entries]], axis=1)
        .reshape(node_count, entries)
        .astype(jnp.int32)
    )
    wanted = listed // tile_count == lax.axis_index("nodes")
    before = jnp.dot(
        wanted.astype(jnp.bfloat16),
        earlier.T.astype(jnp.bfloat16),
        preferred_element_type=jnp.float32,
    )
    marked = jnp.where(wanted, listed % tile_count + 1, 0)
    incoming = (
        jnp.stack(
            [jnp.sum(jnp.where(before == r, marked, 0), axis=1) for r in range(CAP)], axis=1
        ).reshape(-1)
        - 1
    )

    y_rows = jnp.dot(full_rows, w_gcn, preferred_element_type=jnp.float32).astype(jnp.bfloat16)
    picked = pick_tiles(
        jnp.maximum(incoming, 0), y_rows.reshape(tile_count, tile_rows_n, head_width)
    )
    fetched = lax.all_to_all(
        picked.reshape(exchange_shape), "nodes", split_axis=0, concat_axis=0, tiled=True
    ).reshape(outgoing.shape)
    x_query = summed[:depth, :head_width]
    x_key = summed[:depth, head_width:]
    x_value = summed[depth : 2 * depth, :head_width]
    x_grad = summed[depth : 2 * depth, head_width:]
    kv_state = summed[2 * depth : 2 * depth + head_width, :head_width]
    pq_state = summed[2 * depth : 2 * depth + head_width, head_width:]
    sq_sum = lists[0, entries]
    sk_sum = lists[0, entries + 1]
    scale_grad = jnp.sum(pq_state * kv_state)
    attn_scale = jnp.sqrt(total_rows) / jnp.sqrt(sq_sum * sk_sum + epsilon)
    dm_state = attn_scale * pq_state
    denominator = sq_sum * sk_sum + epsilon
    gq_coef = -0.5 * scale_grad * attn_scale * sk_sum / denominator
    gk_coef = -0.5 * scale_grad * attn_scale * sq_sum / denominator
    grad_qkv = jnp.concatenate(
        [
            attn_scale * jnp.dot(x_grad, kv_state.T, precision=HIGHEST)
            + 2.0 * gq_coef * x_query,
            jnp.dot(x_value, dm_state.T, precision=HIGHEST) + 2.0 * gk_coef * x_key,
            x_grad + jnp.dot(x_key, dm_state, precision=HIGHEST),
        ],
        axis=1,
    )

    mix_rows = jnp.dot(query_full, kv_state, precision=HIGHEST)
    base = value_full + attn_scale * mix_rows + y_rows.astype(jnp.float32)
    dq_rows = (
        attn_scale * jnp.dot(grad_full, kv_state.T, precision=HIGHEST)
        + 2.0 * gq_coef * query_full
    )
    dk_rows = jnp.dot(value_full, dm_state.T, precision=HIGHEST) + 2.0 * gk_coef * key_full
    dv_rows = grad_full + jnp.dot(key_full, dm_state, precision=HIGHEST)
    dqkv = jnp.concatenate([dq_rows, dk_rows, dv_rows], axis=1).astype(jnp.bfloat16)

    dy_rows = add_returned(incoming, returned, grad_tiles).reshape(row_count, head_width)
    gcn_local = contract_rows(full_rows, dy_rows)
    gcn_sent = jnp.concatenate([gcn_local[: depth // 2], gcn_local[depth // 2 :]], axis=1)
    gcn_summed = sum_nodes(gcn_sent, 1)
    partial_grad = lax.dot_general(
        dqkv, w_qkv, (((1,), (1,)), ((), ())), preferred_element_type=jnp.float32
    )
    partial_grad = partial_grad + lax.dot_general(
        dy_rows, w_gcn, (((1,), (1,)), ((), ())), preferred_element_type=jnp.float32
    )
    grad_x = lax.psum_scatter(
        partial_grad.astype(jnp.bfloat16), "feat", scatter_dimension=1, tiled=True
    )
    base, gcn_summed = lax.optimization_barrier((base, gcn_summed))
    mixed = finish_mixed(
        slot_index, fetched, adj_all, base.reshape(tile_count, tile_rows_n, head_width)
    )
    grad_gcn = jnp.concatenate([gcn_summed[:, :head_width], gcn_summed[:, head_width:]], axis=0)
    mixed_tiles = mixed.reshape(tile_count, 1, tile_rows_n * head_width)
    grad_x_tiles = grad_x.reshape(tile_count, 1, tile_rows_n * head_width)
    return (mixed_tiles, grad_x_tiles, grad_qkv, grad_gcn)


def solution(mesh):
    in_specs = (
        P("nodes", "feat", None),
        P(None, "feat"),
        P(None, "feat"),
        P("nodes", None),
        P("nodes", None),
        P("nodes", "feat", None, None),
        P("nodes", "feat", None),
    )
    out_specs = (
        P("nodes", "feat", None),
        P("nodes", "feat", None),
        P(None, "feat"),
        P(None, "feat"),
    )
    return jax.shard_map(local, mesh=mesh, in_specs=in_specs, out_specs=out_specs, check_vma=False)
```

```python
import jax
import jax.numpy as jnp
from jax import lax
from jax.experimental import pallas as pl
from jax.experimental.pallas import tpu as pltpu
from jax.sharding import PartitionSpec as P

epsilon = 1e-06
HIGHEST = lax.Precision.HIGHEST
SIDE = 8
CAP = 2
SUM_BYTES = 100_000_000


def contract_rows(left, right):
    return lax.dot_general(
        left, right, (((0,), (0,)), ((), ())), preferred_element_type=jnp.float32
    )


def sum_kernel(
    x_ref, o_ref, core_buf, half_buf, y_buf, piece_buf, z_buf, total, send_core, recv_core,
    send_y, recv_y, send_z, recv_z, send_g, recv_g, send_last, recv_last,
):
    rows = x_ref.shape[0]
    half = rows // 2
    piece = half // SIDE
    me = lax.axis_index("nodes")
    core = lax.rem(me, 2)
    z = lax.rem(me // 2, SIDE)
    y = me // (2 * SIDE)
    partner = me + 1 - 2 * core

    def at_y(k):
        other = lax.rem(y + k, SIDE)
        return other, (other * SIDE + z) * 2 + core

    def at_z(k):
        other = lax.rem(z + k, SIDE)
        return other, (y * SIDE + other) * 2 + core

    barrier = pltpu.get_barrier_semaphore()
    pl.semaphore_signal(barrier, inc=1, device_id={"nodes": partner})
    for k in range(1, SIDE):
        pl.semaphore_signal(barrier, inc=1, device_id={"nodes": at_y(k)[1]})
        pl.semaphore_signal(barrier, inc=1, device_id={"nodes": at_z(k)[1]})
    pl.semaphore_wait(barrier, 2 * SIDE - 1)

    def block(start, size):
        return pl.ds(pl.multiple_of(start, 8), size)

    copies = []

    def send(src, dst, send_sem, recv_sem, target):
        copy = pltpu.make_async_remote_copy(
            src_ref=src, dst_ref=dst, send_sem=send_sem, recv_sem=recv_sem,
            device_id={"nodes": target},
        )
        copy.start()
        copies.append(copy)
        return copy

    first = send(
        x_ref.at[block((1 - core) * half, half)], core_buf, send_core, recv_core, partner
    )
    first.wait_recv()
    half_buf[...] = x_ref[block(core * half, half), :] + core_buf[...]

    stage = []
    for k in range(1, SIDE):
        other, target = at_y(k)
        stage.append(
            send(
                half_buf.at[block(other * piece, piece)], y_buf.at[y],
                send_y.at[k - 1], recv_y.at[k - 1], target,
            )
        )
    y_buf[y] = half_buf[block(y * piece, piece), :]
    for copy in stage:
        copy.wait_recv()
    acc = y_buf[0]
    for k in range(1, SIDE):
        acc = acc + y_buf[k]
    piece_buf[...] = acc

    stage = []
    for k in range(1, SIDE):
        other, target = at_z(k)
        stage.append(
            send(piece_buf, z_buf.at[z], send_z.at[k - 1], recv_z.at[k - 1], target)
        )
    z_buf[z] = acc
    for copy in stage:
        copy.wait_recv()
    acc = z_buf[0]
    for k in range(1, SIDE):
        acc = acc + z_buf[k]
    mine = block(core * half + y * piece, piece)
    total[mine, :] = acc

    stage = []
    for k in range(1, SIDE):
        other, target = at_y(k)
        stage.append(
            send(total.at[mine], total.at[mine], send_g.at[k - 1], recv_g.at[k - 1], target)
        )
    for copy in stage:
        copy.wait_recv()

    whole = block(core * half, half)
    last = send(total.at[whole], total.at[whole], send_last, recv_last, partner)
    last.wait_recv()
    for copy in copies:
        copy.wait_send()
    o_ref[...] = total[...]


def sum_nodes(x, collective_id):
    rows, lanes = x.shape
    half = rows // 2
    piece = half // SIDE
    f32 = jnp.float32
    dma = pltpu.SemaphoreType.DMA
    return pl.pallas_call(
        sum_kernel,
        out_shape=jax.ShapeDtypeStruct((rows, lanes), f32),
        in_specs=[pl.BlockSpec(memory_space=pltpu.VMEM)],
        out_specs=pl.BlockSpec(memory_space=pltpu.VMEM),
        scratch_shapes=[
            pltpu.VMEM((half, lanes), f32),
            pltpu.VMEM((half, lanes), f32),
            pltpu.VMEM((SIDE, piece, lanes), f32),
            pltpu.VMEM((piece, lanes), f32),
            pltpu.VMEM((SIDE, piece, lanes), f32),
            pltpu.VMEM((rows, lanes), f32),
            dma, dma,
            dma((SIDE - 1,)), dma((SIDE - 1,)),
            dma((SIDE - 1,)), dma((SIDE - 1,)),
            dma((SIDE - 1,)), dma((SIDE - 1,)),
            dma, dma,
        ],
        compiler_params=pltpu.CompilerParams(
            collective_id=collective_id, has_side_effects=True
        ),
        cost_estimate=pl.CostEstimate(
            flops=0, bytes_accessed=SUM_BYTES, transcendentals=0
        ),
        name="sum_nodes",
    )(x)


def pack(tile):
    half = tile.shape[0] // 2
    return jnp.concatenate([tile[:half], tile[half:]], axis=1)


def unpack(tile):
    half = tile.shape[1] // 2
    return jnp.concatenate([tile[:, :half], tile[:, half:]], axis=0)


def back_kernel(slot_ref, grad_ref, *rest):
    adj_refs, (out_ref, terms, sem) = rest[:-3], rest[-3:]
    tiles, width = grad_ref.shape[0], len(adj_refs)

    def one_tile(t, carry):
        grad = grad_ref[t]
        for n in range(width):
            term = lax.dot_general(
                adj_refs[n][t], grad, (((0,), (0,)), ((), ())),
                preferred_element_type=jnp.float32,
            )
            j = t * width + n
            terms[j] = pack(term).astype(jnp.bfloat16)
        return carry

    lax.fori_loop(0, tiles, one_tile, 0, unroll=4)

    def place(j, carry):
        pltpu.make_async_copy(terms.at[j], out_ref.at[slot_ref[j]], sem).start()
        return carry

    lax.fori_loop(0, tiles * width, place, 0)
    pltpu.make_async_copy(terms, out_ref.at[pl.ds(0, tiles * width)], sem).wait()


def place_back_terms(slot_index, adj_all, grad_tiles, slots):
    width = len(adj_all)
    tiles, rows, columns = grad_tiles.shape
    packed = (rows // 2, columns * 2)
    return pl.pallas_call(
        back_kernel,
        out_shape=jax.ShapeDtypeStruct((slots,) + packed, jnp.bfloat16),
        in_specs=[
            pl.BlockSpec(memory_space=pltpu.SMEM),
            pl.BlockSpec(memory_space=pltpu.VMEM),
        ]
        + [pl.BlockSpec(memory_space=pltpu.VMEM)] * width,
        out_specs=pl.BlockSpec(memory_space=pl.ANY),
        scratch_shapes=[
            pltpu.VMEM((tiles * width,) + packed, jnp.bfloat16),
            pltpu.SemaphoreType.DMA,
        ],
        name="place_back_terms",
    )(slot_index, grad_tiles, *adj_all)


def pick_kernel(id_ref, y_ref, out_ref, packed_ref, sem):
    for t in range(y_ref.shape[0]):
        packed_ref[t] = pack(y_ref[t].astype(jnp.float32)).astype(jnp.bfloat16)

    def place(j, carry):
        pltpu.make_async_copy(packed_ref.at[id_ref[j]], out_ref.at[j], sem).start()
        return carry

    lax.fori_loop(0, out_ref.shape[0], place, 0)
    pltpu.make_async_copy(out_ref, out_ref, sem).wait()


def pick_tiles(ids, y_tiles):
    tiles, rows, columns = y_tiles.shape
    packed = (rows // 2, columns * 2)
    return pl.pallas_call(
        pick_kernel,
        out_shape=jax.ShapeDtypeStruct((ids.shape[0],) + packed, jnp.bfloat16),
        in_specs=[
            pl.BlockSpec(memory_space=pltpu.SMEM),
            pl.BlockSpec(memory_space=pltpu.VMEM),
        ],
        out_specs=pl.BlockSpec(memory_space=pl.ANY),
        scratch_shapes=[
            pltpu.VMEM((tiles,) + packed, jnp.bfloat16),
            pltpu.SemaphoreType.DMA,
        ],
        name="pick_tiles",
    )(ids, y_tiles)


def add_kernel(id_ref, returned_ref, grad_ref, dy_ref, acc):
    acc[...] = jnp.zeros_like(acc)

    def add(j, carry):
        tile = id_ref[j]

        @pl.when(tile >= 0)
        def _():
            acc[tile] = acc[tile] + returned_ref[j].astype(jnp.float32)

        return carry

    lax.fori_loop(0, returned_ref.shape[0], add, 0)
    for t in range(grad_ref.shape[0]):
        total = grad_ref[t].astype(jnp.float32) + unpack(acc[t])
        dy_ref[t] = total.astype(jnp.bfloat16)


def add_returned(ids, returned, grad_tiles):
    tiles, rows, columns = grad_tiles.shape
    return pl.pallas_call(
        add_kernel,
        out_shape=jax.ShapeDtypeStruct(grad_tiles.shape, jnp.bfloat16),
        in_specs=[
            pl.BlockSpec(memory_space=pltpu.SMEM),
            pl.BlockSpec(memory_space=pltpu.VMEM),
            pl.BlockSpec(memory_space=pltpu.VMEM),
        ],
        out_specs=pl.BlockSpec(memory_space=pltpu.VMEM),
        scratch_shapes=[pltpu.VMEM((tiles, rows // 2, columns * 2), jnp.float32)],
        name="add_returned",
    )(ids, returned, grad_tiles)


def mixed_kernel(slot_ref, fetched_ref, base_ref, *rest):
    adj_refs, (out_ref, held, sem) = rest[:-3], rest[-3:]
    tiles, width = base_ref.shape[0], len(adj_refs)

    def fetch(j, carry):
        pltpu.make_async_copy(fetched_ref.at[slot_ref[j]], held.at[j], sem).start()
        return carry

    lax.fori_loop(0, tiles * width, fetch, 0)
    pltpu.make_async_copy(fetched_ref.at[pl.ds(0, tiles * width)], held, sem).wait()

    def one_tile(t, carry):
        acc = base_ref[t]
        for n in range(width):
            rows = unpack(held[t * width + n].astype(jnp.float32)).astype(jnp.bfloat16)
            acc = acc + jnp.dot(adj_refs[n][t], rows, preferred_element_type=jnp.float32)
        out_ref[t] = acc.astype(jnp.bfloat16)
        return carry

    lax.fori_loop(0, tiles, one_tile, 0, unroll=4)


def finish_mixed(slot_index, fetched, adj_all, base):
    tiles, width = base.shape[0], len(adj_all)
    return pl.pallas_call(
        mixed_kernel,
        out_shape=jax.ShapeDtypeStruct(base.shape, jnp.bfloat16),
        in_specs=[
            pl.BlockSpec(memory_space=pltpu.SMEM),
            pl.BlockSpec(memory_space=pl.ANY),
            pl.BlockSpec(memory_space=pltpu.VMEM),
        ]
        + [pl.BlockSpec(memory_space=pltpu.VMEM)] * width,
        out_specs=pl.BlockSpec(memory_space=pltpu.VMEM),
        scratch_shapes=[
            pltpu.VMEM((tiles * width,) + fetched.shape[1:], jnp.bfloat16),
            pltpu.SemaphoreType.DMA,
        ],
        name="finish_mixed",
    )(slot_index, fetched, base, *adj_all)


def shifted(block, shift):
    count = lax.axis_size("feat")
    return lax.ppermute(block, "feat", [(i, (i + shift) % count) for i in range(count)])


def relative(rows):
    count = lax.axis_size("feat")
    size = rows.shape[0] // count
    me = lax.axis_index("feat")
    return jnp.concatenate(
        [
            lax.dynamic_slice_in_dim(rows, lax.rem(me - k + count, count) * size, size, axis=0)
            for k in range(count)
        ],
        axis=0,
    )


def local(feats, w_qkv, w_gcn, nbr_owner, nbr_tile, adj_blocks, grad_out):
    tile_count = nbr_owner.shape[0]
    list_width = nbr_owner.shape[1]
    head_width = w_gcn.shape[1]
    tile_rows_n = feats.shape[2] // head_width
    row_count = tile_count * tile_rows_n
    node_count = lax.axis_size("nodes")
    slots = node_count * CAP
    entries = tile_count * list_width
    total_rows = jnp.float32(row_count * node_count)
    feat_count = lax.axis_size("feat")
    w_qkv = relative(w_qkv)
    w_gcn = relative(w_gcn)
    own_feats = feats.reshape(tile_count, -1)
    others = [shifted(own_feats, k) for k in range(1, feat_count)]
    others, adj_own = lax.optimization_barrier(
        (others, adj_blocks.reshape(tile_count, tile_rows_n, tile_rows_n))
    )
    adj_all = [adj_own] + [shifted(adj_own, k) for k in range(1, feat_count)]
    full_rows = jnp.concatenate(
        [block.reshape(row_count, head_width) for block in [own_feats] + others], axis=1
    )
    grad_tiles = grad_out.reshape(tile_count, tile_rows_n, head_width)
    grad_rows = grad_tiles.reshape(row_count, head_width)

    owners = nbr_owner.reshape(-1)
    place = jnp.arange(entries, dtype=jnp.int32)
    earlier = place[:, None] > place[None, :]
    same = owners[:, None] == owners[None, :]
    rank_within = jnp.sum((earlier & same).astype(jnp.int32), axis=1)
    slots_listed = (owners * CAP + rank_within).reshape(tile_count, list_width)
    order = lax.rem(lax.axis_index("feat") - jnp.arange(list_width) + list_width, list_width)
    picks = order[:, None] == jnp.arange(list_width)[None, :]
    slot_index = jnp.sum(
        jnp.where(picks[None], slots_listed[:, None, :], 0), axis=2
    ).reshape(-1)

    proj = jnp.dot(full_rows, w_qkv, preferred_element_type=jnp.float32).astype(jnp.bfloat16)
    query_rows = proj[:, :head_width]
    key_rows = proj[:, head_width : 2 * head_width]
    value_rows = proj[:, 2 * head_width :]
    query_full = query_rows.astype(jnp.float32)
    key_full = key_rows.astype(jnp.float32)
    value_full = value_rows.astype(jnp.float32)
    grad_full = grad_rows.astype(jnp.float32)
    sq_local = jnp.sum(query_full * query_full)
    sk_local = jnp.sum(key_full * key_full)
    kv_local = contract_rows(key_rows, value_rows)
    pq_local = contract_rows(query_rows, grad_rows)
    stacked = jnp.concatenate([proj, grad_rows], axis=1)
    x_local = contract_rows(full_rows, stacked)
    depth = x_local.shape[0]
    lanes = 2 * head_width
    me = lax.axis_index("nodes")
    codes = jnp.pad(
        (nbr_owner * tile_count + nbr_tile).reshape(-1).astype(jnp.float32),
        (0, head_width - entries),
    )
    list_row = lax.broadcasted_iota(jnp.int32, (node_count // 2, lanes), 0)
    list_lane = lax.broadcasted_iota(jnp.int32, (node_count // 2, lanes), 1)
    mine = (list_row == me // 2) & (list_lane // head_width == me % 2)
    own_list = jnp.where(mine, jnp.tile(codes, 2)[None, :], 0.0)
    first = list_row == 0
    own_list = own_list + jnp.where(first & (list_lane == entries), sq_local, 0.0)
    own_list = own_list + jnp.where(first & (list_lane == entries + 1), sk_local, 0.0)
    sent = jnp.concatenate(
        [
            x_local[:, :lanes],
            x_local[:, lanes:],
            jnp.concatenate([kv_local, pq_local], axis=1),
            own_list,
        ],
        axis=0,
    )
    summed = sum_nodes(sent, 0)
    summed, adj_all = lax.optimization_barrier((summed, adj_all))
    outgoing = place_back_terms(slot_index, adj_all, grad_tiles, slots)
    exchange_shape = (node_count, CAP) + outgoing.shape[1:]
    returned = lax.all_to_all(
        outgoing.reshape(exchange_shape), "nodes", split_axis=0, concat_axis=0, tiled=True
    ).reshape(outgoing.shape)

    lists = summed[2 * depth + head_width :]
    listed = (
        jnp.stack([lists[:, :entries], lists[:, head_width : head_width + entries]], axis=1)
        .reshape(node_count, entries)
        .astype(jnp.int32)
    )
    wanted = listed // tile_count == lax.axis_index("nodes")
    before = jnp.dot(
        wanted.astype(jnp.bfloat16),
        earlier.T.astype(jnp.bfloat16),
        preferred_element_type=jnp.float32,
    )
    marked = jnp.where(wanted, listed % tile_count + 1, 0)
    incoming = (
        jnp.stack(
            [jnp.sum(jnp.where(before == r, marked, 0), axis=1) for r in range(CAP)], axis=1
        ).reshape(-1)
        - 1
    )

    y_rows = jnp.dot(full_rows, w_gcn, preferred_element_type=jnp.float32).astype(jnp.bfloat16)
    picked = pick_tiles(
        jnp.maximum(incoming, 0), y_rows.reshape(tile_count, tile_rows_n, head_width)
    )
    fetched = lax.all_to_all(
        picked.reshape(exchange_shape), "nodes", split_axis=0, concat_axis=0, tiled=True
    ).reshape(outgoing.shape)
    x_query = summed[:depth, :head_width]
    x_key = summed[:depth, head_width:]
    x_value = summed[depth : 2 * depth, :head_width]
    x_grad = summed[depth : 2 * depth, head_width:]
    kv_state = summed[2 * depth : 2 * depth + head_width, :head_width]
    pq_state = summed[2 * depth : 2 * depth + head_width, head_width:]
    sq_sum = lists[0, entries]
    sk_sum = lists[0, entries + 1]
    scale_grad = jnp.sum(pq_state * kv_state)
    attn_scale = jnp.sqrt(total_rows) / jnp.sqrt(sq_sum * sk_sum + epsilon)
    dm_state = attn_scale * pq_state
    denominator = sq_sum * sk_sum + epsilon
    gq_coef = -0.5 * scale_grad * attn_scale * sk_sum / denominator
    gk_coef = -0.5 * scale_grad * attn_scale * sq_sum / denominator
    grad_qkv = jnp.concatenate(
        [
            attn_scale * jnp.dot(x_grad, kv_state.T, precision=HIGHEST)
            + 2.0 * gq_coef * x_query,
            jnp.dot(x_value, dm_state.T, precision=HIGHEST) + 2.0 * gk_coef * x_key,
            x_grad + jnp.dot(x_key, dm_state, precision=HIGHEST),
        ],
        axis=1,
    )

    grad_qkv = relative(grad_qkv)
    mix_rows = jnp.dot(query_full, kv_state, precision=HIGHEST)
    base = value_full + attn_scale * mix_rows + y_rows.astype(jnp.float32)
    dq_rows = (
        attn_scale * jnp.dot(grad_full, kv_state.T, precision=HIGHEST)
        + 2.0 * gq_coef * query_full
    )
    dk_rows = jnp.dot(value_full, dm_state.T, precision=HIGHEST) + 2.0 * gk_coef * key_full
    dv_rows = grad_full + jnp.dot(key_full, dm_state, precision=HIGHEST)
    dqkv = jnp.concatenate([dq_rows, dk_rows, dv_rows], axis=1).astype(jnp.bfloat16)

    dy_rows = add_returned(incoming, returned, grad_tiles).reshape(row_count, head_width)
    gcn_local = relative(contract_rows(full_rows, dy_rows))
    gcn_sent = jnp.concatenate([gcn_local[: depth // 2], gcn_local[depth // 2 :]], axis=1)
    partial_grad = lax.dot_general(
        dqkv, w_qkv, (((1,), (1,)), ((), ())), preferred_element_type=jnp.float32
    )
    partial_grad = partial_grad + lax.dot_general(
        dy_rows, w_gcn, (((1,), (1,)), ((), ())), preferred_element_type=jnp.float32
    )
    pieces = [
        partial_grad[:, k * head_width : (k + 1) * head_width].astype(jnp.bfloat16)
        for k in range(feat_count)
    ]
    grad_x = pieces[0].astype(jnp.float32)
    for k in range(1, feat_count):
        grad_x = grad_x + shifted(pieces[k], -k).astype(jnp.float32)
    grad_x = grad_x.astype(jnp.bfloat16)
    grad_x = grad_x.reshape(tile_count, 1, tile_rows_n * head_width)
    grad_x, gcn_sent = lax.optimization_barrier((grad_x, gcn_sent))
    gcn_summed = sum_nodes(gcn_sent, 1)
    base, gcn_summed = lax.optimization_barrier((base, gcn_summed))
    mixed = finish_mixed(
        slot_index, fetched, adj_all, base.reshape(tile_count, tile_rows_n, head_width)
    )
    grad_gcn = jnp.concatenate([gcn_summed[:, :head_width], gcn_summed[:, head_width:]], axis=0)
    mixed_tiles = mixed.reshape(tile_count, 1, tile_rows_n * head_width)
    return (mixed_tiles, grad_x, grad_qkv, grad_gcn)


def solution(mesh):
    in_specs = (
        P("nodes", "feat", None),
        P(None, "feat"),
        P(None, "feat"),
        P("nodes", None),
        P("nodes", None),
        P("nodes", "feat", None, None),
        P("nodes", "feat", None),
    )
    out_specs = (
        P("nodes", "feat", None),
        P("nodes", "feat", None),
        P(None, "feat"),
        P(None, "feat"),
    )
    return jax.shard_map(local, mesh=mesh, in_specs=in_specs, out_specs=out_specs, check_vma=False)
```

```python
import jax
import jax.numpy as jnp
from jax import lax
from jax.experimental import pallas as pl
from jax.experimental.pallas import tpu as pltpu
from jax.sharding import PartitionSpec as P

epsilon = 1e-06
HIGHEST = lax.Precision.HIGHEST
SIDE = 8
CAP = 2
SUM_BYTES = 100_000_000


def contract_rows(left, right):
    return lax.dot_general(
        left, right, (((0,), (0,)), ((), ())), preferred_element_type=jnp.float32
    )


def sum_kernel(
    x_ref, o_ref, core_buf, half_buf, y_buf, piece_buf, z_buf, total, send_core, recv_core,
    send_y, recv_y, send_z, recv_z, send_g, recv_g, send_last, recv_last,
):
    rows = x_ref.shape[0]
    half = rows // 2
    piece = half // SIDE
    me = lax.axis_index("nodes")
    core = lax.rem(me, 2)
    z = lax.rem(me // 2, SIDE)
    y = me // (2 * SIDE)
    partner = me + 1 - 2 * core

    def at_y(k):
        other = lax.rem(y + k, SIDE)
        return other, (other * SIDE + z) * 2 + core

    def at_z(k):
        other = lax.rem(z + k, SIDE)
        return other, (y * SIDE + other) * 2 + core

    barrier = pltpu.get_barrier_semaphore()
    pl.semaphore_signal(barrier, inc=1, device_id={"nodes": partner})
    for k in range(1, SIDE):
        pl.semaphore_signal(barrier, inc=1, device_id={"nodes": at_y(k)[1]})
        pl.semaphore_signal(barrier, inc=1, device_id={"nodes": at_z(k)[1]})
    pl.semaphore_wait(barrier, 2 * SIDE - 1)

    def block(start, size):
        return pl.ds(pl.multiple_of(start, 8), size)

    copies = []

    def send(src, dst, send_sem, recv_sem, target):
        copy = pltpu.make_async_remote_copy(
            src_ref=src, dst_ref=dst, send_sem=send_sem, recv_sem=recv_sem,
            device_id={"nodes": target},
        )
        copy.start()
        copies.append(copy)
        return copy

    first = send(
        x_ref.at[block((1 - core) * half, half)], core_buf, send_core, recv_core, partner
    )
    first.wait_recv()
    half_buf[...] = x_ref[block(core * half, half), :] + core_buf[...]

    stage = []
    for k in range(1, SIDE):
        other, target = at_y(k)
        stage.append(
            send(
                half_buf.at[block(other * piece, piece)], y_buf.at[y],
                send_y.at[k - 1], recv_y.at[k - 1], target,
            )
        )
    y_buf[y] = half_buf[block(y * piece, piece), :]
    for copy in stage:
        copy.wait_recv()
    acc = y_buf[0]
    for k in range(1, SIDE):
        acc = acc + y_buf[k]
    piece_buf[...] = acc

    stage = []
    for k in range(1, SIDE):
        other, target = at_z(k)
        stage.append(
            send(piece_buf, z_buf.at[z], send_z.at[k - 1], recv_z.at[k - 1], target)
        )
    z_buf[z] = acc
    for copy in stage:
        copy.wait_recv()
    acc = z_buf[0]
    for k in range(1, SIDE):
        acc = acc + z_buf[k]
    mine = block(core * half + y * piece, piece)
    total[mine, :] = acc

    stage = []
    for k in range(1, SIDE):
        other, target = at_y(k)
        stage.append(
            send(total.at[mine], total.at[mine], send_g.at[k - 1], recv_g.at[k - 1], target)
        )
    for copy in stage:
        copy.wait_recv()

    whole = block(core * half, half)
    last = send(total.at[whole], total.at[whole], send_last, recv_last, partner)
    last.wait_recv()
    for copy in copies:
        copy.wait_send()
    o_ref[...] = total[...]


def sum_nodes(x, collective_id):
    rows, lanes = x.shape
    half = rows // 2
    piece = half // SIDE
    f32 = jnp.float32
    dma = pltpu.SemaphoreType.DMA
    return pl.pallas_call(
        sum_kernel,
        out_shape=jax.ShapeDtypeStruct((rows, lanes), f32),
        in_specs=[pl.BlockSpec(memory_space=pltpu.VMEM)],
        out_specs=pl.BlockSpec(memory_space=pltpu.VMEM),
        scratch_shapes=[
            pltpu.VMEM((half, lanes), f32),
            pltpu.VMEM((half, lanes), f32),
            pltpu.VMEM((SIDE, piece, lanes), f32),
            pltpu.VMEM((piece, lanes), f32),
            pltpu.VMEM((SIDE, piece, lanes), f32),
            pltpu.VMEM((rows, lanes), f32),
            dma, dma,
            dma((SIDE - 1,)), dma((SIDE - 1,)),
            dma((SIDE - 1,)), dma((SIDE - 1,)),
            dma((SIDE - 1,)), dma((SIDE - 1,)),
            dma, dma,
        ],
        compiler_params=pltpu.CompilerParams(
            collective_id=collective_id, has_side_effects=True
        ),
        cost_estimate=pl.CostEstimate(
            flops=0, bytes_accessed=SUM_BYTES, transcendentals=0
        ),
        name="sum_nodes",
    )(x)


def pack(tile):
    half = tile.shape[0] // 2
    return jnp.concatenate([tile[:half], tile[half:]], axis=1)


def unpack(tile):
    half = tile.shape[1] // 2
    return jnp.concatenate([tile[:, :half], tile[:, half:]], axis=0)


def back_kernel(slot_ref, grad_ref, *rest):
    adj_refs, (out_ref, terms, sem) = rest[:-3], rest[-3:]
    tiles, width = grad_ref.shape[0], len(adj_refs)

    def one_tile(t, carry):
        grad = grad_ref[t]
        for n in range(width):
            term = lax.dot_general(
                adj_refs[n][t], grad, (((0,), (0,)), ((), ())),
                preferred_element_type=jnp.float32,
            )
            j = t * width + n
            terms[j] = pack(term).astype(jnp.bfloat16)
        return carry

    lax.fori_loop(0, tiles, one_tile, 0, unroll=4)

    def place(j, carry):
        pltpu.make_async_copy(terms.at[j], out_ref.at[slot_ref[j]], sem).start()
        return carry

    lax.fori_loop(0, tiles * width, place, 0)
    pltpu.make_async_copy(terms, out_ref.at[pl.ds(0, tiles * width)], sem).wait()


def place_back_terms(slot_index, adj_all, grad_tiles, slots):
    width = len(adj_all)
    tiles, rows, columns = grad_tiles.shape
    packed = (rows // 2, columns * 2)
    return pl.pallas_call(
        back_kernel,
        out_shape=jax.ShapeDtypeStruct((slots,) + packed, jnp.bfloat16),
        in_specs=[
            pl.BlockSpec(memory_space=pltpu.SMEM),
            pl.BlockSpec(memory_space=pltpu.VMEM),
        ]
        + [pl.BlockSpec(memory_space=pltpu.VMEM)] * width,
        out_specs=pl.BlockSpec(memory_space=pl.ANY),
        scratch_shapes=[
            pltpu.VMEM((tiles * width,) + packed, jnp.bfloat16),
            pltpu.SemaphoreType.DMA,
        ],
        name="place_back_terms",
    )(slot_index, grad_tiles, *adj_all)


def pick_kernel(id_ref, y_ref, out_ref, packed_ref, sem):
    for t in range(y_ref.shape[0]):
        packed_ref[t] = pack(y_ref[t].astype(jnp.float32)).astype(jnp.bfloat16)

    def place(j, carry):
        pltpu.make_async_copy(packed_ref.at[id_ref[j]], out_ref.at[j], sem).start()
        return carry

    lax.fori_loop(0, out_ref.shape[0], place, 0)
    pltpu.make_async_copy(out_ref, out_ref, sem).wait()


def pick_tiles(ids, y_tiles):
    tiles, rows, columns = y_tiles.shape
    packed = (rows // 2, columns * 2)
    return pl.pallas_call(
        pick_kernel,
        out_shape=jax.ShapeDtypeStruct((ids.shape[0],) + packed, jnp.bfloat16),
        in_specs=[
            pl.BlockSpec(memory_space=pltpu.SMEM),
            pl.BlockSpec(memory_space=pltpu.VMEM),
        ],
        out_specs=pl.BlockSpec(memory_space=pl.ANY),
        scratch_shapes=[
            pltpu.VMEM((tiles,) + packed, jnp.bfloat16),
            pltpu.SemaphoreType.DMA,
        ],
        name="pick_tiles",
    )(ids, y_tiles)


def add_kernel(id_ref, returned_ref, grad_ref, dy_ref, acc):
    acc[...] = jnp.zeros_like(acc)

    def add(j, carry):
        tile = id_ref[j]

        @pl.when(tile >= 0)
        def _():
            acc[tile] = acc[tile] + returned_ref[j].astype(jnp.float32)

        return carry

    lax.fori_loop(0, returned_ref.shape[0], add, 0)
    for t in range(grad_ref.shape[0]):
        total = grad_ref[t].astype(jnp.float32) + unpack(acc[t])
        dy_ref[t] = total.astype(jnp.bfloat16)


def add_returned(ids, returned, grad_tiles):
    tiles, rows, columns = grad_tiles.shape
    return pl.pallas_call(
        add_kernel,
        out_shape=jax.ShapeDtypeStruct(grad_tiles.shape, jnp.bfloat16),
        in_specs=[
            pl.BlockSpec(memory_space=pltpu.SMEM),
            pl.BlockSpec(memory_space=pltpu.VMEM),
            pl.BlockSpec(memory_space=pltpu.VMEM),
        ],
        out_specs=pl.BlockSpec(memory_space=pltpu.VMEM),
        scratch_shapes=[pltpu.VMEM((tiles, rows // 2, columns * 2), jnp.float32)],
        name="add_returned",
    )(ids, returned, grad_tiles)


def mixed_kernel(slot_ref, fetched_ref, base_ref, *rest):
    adj_refs, (out_ref, held, sem) = rest[:-3], rest[-3:]
    tiles, width = base_ref.shape[0], len(adj_refs)

    def fetch(j, carry):
        pltpu.make_async_copy(fetched_ref.at[slot_ref[j]], held.at[j], sem).start()
        return carry

    lax.fori_loop(0, tiles * width, fetch, 0)
    pltpu.make_async_copy(fetched_ref.at[pl.ds(0, tiles * width)], held, sem).wait()

    def one_tile(t, carry):
        acc = base_ref[t]
        for n in range(width):
            rows = unpack(held[t * width + n].astype(jnp.float32)).astype(jnp.bfloat16)
            acc = acc + jnp.dot(adj_refs[n][t], rows, preferred_element_type=jnp.float32)
        out_ref[t] = acc.astype(jnp.bfloat16)
        return carry

    lax.fori_loop(0, tiles, one_tile, 0, unroll=4)


def finish_mixed(slot_index, fetched, adj_all, base):
    tiles, width = base.shape[0], len(adj_all)
    return pl.pallas_call(
        mixed_kernel,
        out_shape=jax.ShapeDtypeStruct(base.shape, jnp.bfloat16),
        in_specs=[
            pl.BlockSpec(memory_space=pltpu.SMEM),
            pl.BlockSpec(memory_space=pl.ANY),
            pl.BlockSpec(memory_space=pltpu.VMEM),
        ]
        + [pl.BlockSpec(memory_space=pltpu.VMEM)] * width,
        out_specs=pl.BlockSpec(memory_space=pltpu.VMEM),
        scratch_shapes=[
            pltpu.VMEM((tiles * width,) + fetched.shape[1:], jnp.bfloat16),
            pltpu.SemaphoreType.DMA,
        ],
        name="finish_mixed",
    )(slot_index, fetched, base, *adj_all)


def shifted(block, shift):
    count = lax.axis_size("feat")
    return lax.ppermute(block, "feat", [(i, (i + shift) % count) for i in range(count)])


def relative(rows):
    count = lax.axis_size("feat")
    size = rows.shape[0] // count
    me = lax.axis_index("feat")
    return jnp.concatenate(
        [
            lax.dynamic_slice_in_dim(rows, lax.rem(me - k + count, count) * size, size, axis=0)
            for k in range(count)
        ],
        axis=0,
    )


def local(feats, w_qkv, w_gcn, nbr_owner, nbr_tile, adj_blocks, grad_out):
    tile_count = nbr_owner.shape[0]
    list_width = nbr_owner.shape[1]
    head_width = w_gcn.shape[1]
    tile_rows_n = feats.shape[2] // head_width
    row_count = tile_count * tile_rows_n
    node_count = lax.axis_size("nodes")
    slots = node_count * CAP
    entries = tile_count * list_width
    total_rows = jnp.float32(row_count * node_count)
    feat_count = lax.axis_size("feat")
    w_qkv = relative(w_qkv)
    w_gcn = relative(w_gcn)
    own_feats = feats.reshape(tile_count, -1)
    others = [shifted(own_feats, k) for k in range(1, feat_count)]
    adj_own = adj_blocks.reshape(tile_count, tile_rows_n, tile_rows_n)
    adj_all = [adj_own] + [shifted(adj_own, k) for k in range(1, feat_count)]
    full_rows = jnp.concatenate(
        [block.reshape(row_count, head_width) for block in [own_feats] + others], axis=1
    )
    grad_tiles = grad_out.reshape(tile_count, tile_rows_n, head_width)
    grad_rows = grad_tiles.reshape(row_count, head_width)

    owners = nbr_owner.reshape(-1)
    place = jnp.arange(entries, dtype=jnp.int32)
    earlier = place[:, None] > place[None, :]
    same = owners[:, None] == owners[None, :]
    rank_within = jnp.sum((earlier & same).astype(jnp.int32), axis=1)
    slots_listed = (owners * CAP + rank_within).reshape(tile_count, list_width)
    order = lax.rem(lax.axis_index("feat") - jnp.arange(list_width) + list_width, list_width)
    picks = order[:, None] == jnp.arange(list_width)[None, :]
    slot_index = jnp.sum(
        jnp.where(picks[None], slots_listed[:, None, :], 0), axis=2
    ).reshape(-1)

    proj = jnp.dot(full_rows, w_qkv, preferred_element_type=jnp.float32).astype(jnp.bfloat16)
    query_rows = proj[:, :head_width]
    key_rows = proj[:, head_width : 2 * head_width]
    value_rows = proj[:, 2 * head_width :]
    query_full = query_rows.astype(jnp.float32)
    key_full = key_rows.astype(jnp.float32)
    value_full = value_rows.astype(jnp.float32)
    grad_full = grad_rows.astype(jnp.float32)
    sq_local = jnp.sum(query_full * query_full)
    sk_local = jnp.sum(key_full * key_full)
    kv_local = contract_rows(key_rows, value_rows)
    pq_local = contract_rows(query_rows, grad_rows)
    stacked = jnp.concatenate([proj, grad_rows], axis=1)
    x_local = contract_rows(full_rows, stacked)
    depth = x_local.shape[0]
    lanes = 2 * head_width
    me = lax.axis_index("nodes")
    codes = jnp.pad(
        (nbr_owner * tile_count + nbr_tile).reshape(-1).astype(jnp.float32),
        (0, head_width - entries),
    )
    list_row = lax.broadcasted_iota(jnp.int32, (node_count // 2, lanes), 0)
    list_lane = lax.broadcasted_iota(jnp.int32, (node_count // 2, lanes), 1)
    mine = (list_row == me // 2) & (list_lane // head_width == me % 2)
    own_list = jnp.where(mine, jnp.tile(codes, 2)[None, :], 0.0)
    first = list_row == 0
    own_list = own_list + jnp.where(first & (list_lane == entries), sq_local, 0.0)
    own_list = own_list + jnp.where(first & (list_lane == entries + 1), sk_local, 0.0)
    sent = jnp.concatenate(
        [
            x_local[:, :lanes],
            x_local[:, lanes:],
            jnp.concatenate([kv_local, pq_local], axis=1),
            own_list,
        ],
        axis=0,
    )
    summed = sum_nodes(sent, 0)
    summed, adj_all = lax.optimization_barrier((summed, adj_all))
    outgoing = place_back_terms(slot_index, adj_all, grad_tiles, slots)
    exchange_shape = (node_count, CAP) + outgoing.shape[1:]
    returned = lax.all_to_all(
        outgoing.reshape(exchange_shape), "nodes", split_axis=0, concat_axis=0, tiled=True
    ).reshape(outgoing.shape)

    lists = summed[2 * depth + head_width :]
    listed = (
        jnp.stack([lists[:, :entries], lists[:, head_width : head_width + entries]], axis=1)
        .reshape(node_count, entries)
        .astype(jnp.int32)
    )
    wanted = listed // tile_count == lax.axis_index("nodes")
    before = jnp.dot(
        wanted.astype(jnp.bfloat16),
        earlier.T.astype(jnp.bfloat16),
        preferred_element_type=jnp.float32,
    )
    marked = jnp.where(wanted, listed % tile_count + 1, 0)
    incoming = (
        jnp.stack(
            [jnp.sum(jnp.where(before == r, marked, 0), axis=1) for r in range(CAP)], axis=1
        ).reshape(-1)
        - 1
    )

    y_rows = jnp.dot(full_rows, w_gcn, preferred_element_type=jnp.float32).astype(jnp.bfloat16)
    picked = pick_tiles(
        jnp.maximum(incoming, 0), y_rows.reshape(tile_count, tile_rows_n, head_width)
    )
    fetched = lax.all_to_all(
        picked.reshape(exchange_shape), "nodes", split_axis=0, concat_axis=0, tiled=True
    ).reshape(outgoing.shape)
    x_query = summed[:depth, :head_width]
    x_key = summed[:depth, head_width:]
    x_value = summed[depth : 2 * depth, :head_width]
    x_grad = summed[depth : 2 * depth, head_width:]
    kv_state = summed[2 * depth : 2 * depth + head_width, :head_width]
    pq_state = summed[2 * depth : 2 * depth + head_width, head_width:]
    sq_sum = lists[0, entries]
    sk_sum = lists[0, entries + 1]
    scale_grad = jnp.sum(pq_state * kv_state)
    attn_scale = jnp.sqrt(total_rows) / jnp.sqrt(sq_sum * sk_sum + epsilon)
    dm_state = attn_scale * pq_state
    denominator = sq_sum * sk_sum + epsilon
    gq_coef = -0.5 * scale_grad * attn_scale * sk_sum / denominator
    gk_coef = -0.5 * scale_grad * attn_scale * sq_sum / denominator
    grad_qkv = jnp.concatenate(
        [
            attn_scale * jnp.dot(x_grad, kv_state.T, precision=HIGHEST)
            + 2.0 * gq_coef * x_query,
            jnp.dot(x_value, dm_state.T, precision=HIGHEST) + 2.0 * gk_coef * x_key,
            x_grad + jnp.dot(x_key, dm_state, precision=HIGHEST),
        ],
        axis=1,
    )

    grad_qkv = relative(grad_qkv)
    mix_rows = jnp.dot(query_full, kv_state, precision=HIGHEST)
    base = value_full + attn_scale * mix_rows + y_rows.astype(jnp.float32)
    dq_rows = (
        attn_scale * jnp.dot(grad_full, kv_state.T, precision=HIGHEST)
        + 2.0 * gq_coef * query_full
    )
    dk_rows = jnp.dot(value_full, dm_state.T, precision=HIGHEST) + 2.0 * gk_coef * key_full
    dv_rows = grad_full + jnp.dot(key_full, dm_state, precision=HIGHEST)
    dqkv = jnp.concatenate([dq_rows, dk_rows, dv_rows], axis=1).astype(jnp.bfloat16)

    dy_rows = add_returned(incoming, returned, grad_tiles).reshape(row_count, head_width)
    gcn_local = relative(contract_rows(full_rows, dy_rows))
    gcn_sent = jnp.concatenate([gcn_local[: depth // 2], gcn_local[depth // 2 :]], axis=1)
    partial_grad = lax.dot_general(
        dqkv, w_qkv, (((1,), (1,)), ((), ())), preferred_element_type=jnp.float32
    )
    partial_grad = partial_grad + lax.dot_general(
        dy_rows, w_gcn, (((1,), (1,)), ((), ())), preferred_element_type=jnp.float32
    )
    pieces = [
        partial_grad[:, k * head_width : (k + 1) * head_width].astype(jnp.bfloat16)
        for k in range(feat_count)
    ]
    grad_x = pieces[0].astype(jnp.float32)
    for k in range(1, feat_count):
        grad_x = grad_x + shifted(pieces[k], -k).astype(jnp.float32)
    grad_x = grad_x.astype(jnp.bfloat16)
    grad_x = grad_x.reshape(tile_count, 1, tile_rows_n * head_width)
    grad_x, gcn_sent = lax.optimization_barrier((grad_x, gcn_sent))
    gcn_summed = sum_nodes(gcn_sent, 1)
    base, gcn_summed = lax.optimization_barrier((base, gcn_summed))
    mixed = finish_mixed(
        slot_index, fetched, adj_all, base.reshape(tile_count, tile_rows_n, head_width)
    )
    grad_gcn = jnp.concatenate([gcn_summed[:, :head_width], gcn_summed[:, head_width:]], axis=0)
    mixed_tiles = mixed.reshape(tile_count, 1, tile_rows_n * head_width)
    return (mixed_tiles, grad_x, grad_qkv, grad_gcn)


def solution(mesh):
    in_specs = (
        P("nodes", "feat", None),
        P(None, "feat"),
        P(None, "feat"),
        P("nodes", None),
        P("nodes", None),
        P("nodes", "feat", None, None),
        P("nodes", "feat", None),
    )
    out_specs = (
        P("nodes", "feat", None),
        P("nodes", "feat", None),
        P(None, "feat"),
        P(None, "feat"),
    )
    return jax.shard_map(local, mesh=mesh, in_specs=in_specs, out_specs=out_specs, check_vma=False)
```
